128 devices in a mesh: map: 16 (over y, x), rep: 8 (over z, core).
Axes of the slice: x: 4, y: 4, z: 4, core: 2. Of those that a mesh axis runs over, the one named last changes fastest.
Arguments:
- amplitudes: float32 [2, 4096, 5120], P(None, ('map', 'rep')), may hold values from -6 to 6
- integrals: float32 [2, 5120, 5120], P(None, None, ('map', 'rep')), may hold values from -0.078125 to 0.078125
- row_gap: float32 [2, 4096], P(None, ('map', 'rep')), may hold values from 0.5 to 4
- col_gap: float32 [2, 5120], replicated, may hold values from 0.5 to 4
Outputs:
- update: float32 [2, 4096, 5120], P(None, ('map', 'rep'))
The draws below stay inside these ranges and needn't reach their ends.
All inputs are finite; a program needn't handle non-finite values.
Results may differ from the reference program's by a relative error of at most 0.00007.
Values sent between devices are 32-bit elements; how exact they have to be, the bound alone decides.
No kernel may reach another device: no remote copies, remote signals or barrier semaphores. Data moves between devices by JAX's collectives and lax.ppermute only.
A program may use at most 128 MiB of HBM per device.

```python
import math
import jax
import jax.numpy as jnp
from jax import lax

PAIRS = 5120
BLOCKS = 2
SLAB = 4096


def shard_levels(stream_key, shape, shards, least, largest):
    gain, own = 1.0, jax.random.fold_in(stream_key, 6)
    for dim, parts in shards:
        steps = jnp.exp(jax.random.uniform(jax.random.fold_in(own, dim), (parts,), jnp.float32, least / len(shards), largest / len(shards)))
        gain = gain * jnp.repeat(steps, shape[dim] // parts).reshape([-1 if axis == dim else 1 for axis in range(len(shape))])
    return gain


def noise(stream_key, dims, scale, reach, cuts=(), held_as=jnp.bfloat16):
    drawn = jax.random.normal(stream_key, dims, jnp.float32) * scale
    if len(cuts) > 0:
        drawn = shard_levels(stream_key, dims, cuts, -0.22, 0.18) * drawn
    return jnp.clip(drawn, min=-reach, max=reach).astype(held_as)


def setup_inputs(seed: int = 0) -> dict:
    key_of = jax.random.split(jax.random.key(seed), 5)
    amplitudes = noise(key_of[0], (BLOCKS, SLAB, PAIRS), 1.0, 6.0, ((1, 128),), jnp.float32)
    integrals = noise(key_of[1], (BLOCKS, PAIRS, PAIRS), PAIRS ** -0.5, 0.078125, ((2, 128),), jnp.float32)
    row_gap = jnp.clip(jnp.exp(math.log(4.0) - 2.0794415 * jax.random.uniform(key_of[2], (BLOCKS, SLAB), jnp.float32) ** shard_levels(key_of[2], (BLOCKS, SLAB), ((1, 128),), -0.2, 0.2)), 0.5, 4.0)
    col_gap = jnp.clip(jnp.exp(jax.random.uniform(key_of[3], (BLOCKS, PAIRS), jnp.float32, math.log(0.5), math.log(4.0))), 0.5, 4.0)
    return {"amplitudes": amplitudes, "integrals": integrals, "row_gap": row_gap, "col_gap": col_gap}


def reference(amplitudes, integrals, row_gap, col_gap):
    product = jnp.einsum("gpk,gkq->gpq", amplitudes, integrals, precision=lax.Precision.HIGHEST, preferred_element_type=jnp.float32)
    return product / (row_gap[:, :, None] + col_gap[:, None, :])
```

```python
import jax
import jax.numpy as jnp
from jax import lax
from jax.sharding import PartitionSpec as P

AXES = ("y", "x", "z", "c")
SIDE = 4


def routes(target):
    pairs = []
    for y in range(SIDE):
        for x in range(SIDE):
            for z in range(SIDE):
                for c in range(2):
                    ty, tx, tz, tc = target(y, x, z, c)
                    source = ((y * SIDE + x) * SIDE + z) * 2 + c
                    pairs.append((source, ((ty % SIDE * SIDE + tx % SIDE) * SIDE + tz % SIDE) * 2 + tc % 2))
    return pairs


def along_y(step):
    return routes(lambda y, x, z, c: (y + step, x, z, c))


def along_k(step):
    return routes(lambda y, x, z, c: (y, x, z + step, c) if c == 0 else (y, x + step, z, c))


def along_m(step):
    return routes(lambda y, x, z, c: (y, x + step, z, c) if c == 0 else (y, x, z + step, c))


OTHER_CORE = routes(lambda y, x, z, c: (y, x, z, c + 1))


def send(value, route):
    return lax.ppermute(value, AXES, route)


def contracted_split(rows, k_index):
    depth = rows.shape[1] // SIDE
    blocks = [lax.dynamic_slice_in_dim(rows, (k_index + s) % SIDE * depth, depth, axis=1) for s in range(SIDE)]
    return [blocks[0]] + [send(blocks[s], along_k(s)) for s in range(1, SIDE)]


def ring_gather(block, along):
    half = block.shape[0] // 2
    before = send(block, along(1))
    after = send(block, along(-1))
    far = jnp.concatenate([send(before[:half], along(1)), send(after[half:], along(-1))], axis=0)
    return [block, before, far, after]


def ring_reduce(parts):
    half = parts[0].shape[0] // 2
    low = send(parts[2][:half], along_k(-1))
    high = send(parts[2][half:], along_k(1))
    down = send(jnp.concatenate([parts[1][:half] + low, parts[1][half:]], axis=0), along_k(-1))
    up = send(jnp.concatenate([parts[3][:half], parts[3][half:] + high], axis=0), along_k(1))
    return parts[0] + down + up


def per_device(amplitudes, integrals, row_gap, col_gap):
    y, x, z, c = (lax.axis_index(name) for name in AXES)
    k_index = jnp.where(c == 0, z, x)
    m_index = jnp.where(c == 0, x, z)
    columns = jnp.swapaxes(integrals, 1, 2)

    own_rows = lax.dynamic_index_in_dim(amplitudes, c, 0, keepdims=False)
    other_rows = send(lax.dynamic_index_in_dim(amplitudes, 1 - c, 0, keepdims=False), OTHER_CORE)
    own_columns = lax.dynamic_index_in_dim(columns, c, 0, keepdims=False)
    other_columns = send(lax.dynamic_index_in_dim(columns, 1 - c, 0, keepdims=False), OTHER_CORE)
    rows = jnp.concatenate([own_rows, other_rows], axis=0)
    first = jnp.where(c == 0, own_columns, other_columns)
    second = jnp.where(c == 0, other_columns, own_columns)
    cols = jnp.concatenate([first, second], axis=0)

    amp_blocks = ring_gather(jnp.concatenate(contracted_split(rows, k_index), axis=0), along_y)
    col_blocks = ring_gather(jnp.concatenate(contracted_split(cols, k_index), axis=0), along_m)

    wide = cols.shape[0]
    depth = amp_blocks[0].shape[1]
    relative = jnp.stack(col_blocks).reshape(SIDE, SIDE, wide, depth)
    spread = jnp.zeros((SIDE, SIDE, wide, depth), jnp.float32)
    order = jnp.arange(SIDE)
    by_m = relative[(m_index - order) % SIDE]
    by_mk = by_m[:, (k_index - order) % SIDE]
    xz = jnp.where(c == 0, by_mk, jnp.swapaxes(by_mk, 0, 1)).reshape(SIDE * SIDE * wide, depth)

    pieces = []
    for amp_block in amp_blocks:
        partial = lax.dot_general(
            amp_block, xz, (((1,), (1,)), ((), ())), precision=lax.Precision.HIGH, preferred_element_type=jnp.float32
        )
        pieces.append(ring_reduce(jnp.split(partial, SIDE, axis=0)))
    arrived = [pieces[0]] + [send(pieces[t], along_y(-t)) for t in range(1, SIDE)]
    full = jnp.stack(arrived, axis=0)[(order - y) % SIDE]
    full = jnp.swapaxes(full, 0, 1).reshape(pieces[0].shape[0], -1)
    half = full.shape[0] // 2
    theirs = send(full[half:], OTHER_CORE)
    mine = full[:half]
    product = jnp.stack([jnp.where(c == 0, mine, theirs), jnp.where(c == 0, theirs, mine)])
    return product / (row_gap[:, :, None] + col_gap[:, None, :])


def solution(mesh):
    fine = jax.sharding.Mesh(mesh.devices.reshape(SIDE, SIDE, SIDE, 2), AXES)
    placed = (P(None, AXES, None), P(None, None, AXES), P(None, AXES), P())
    return jax.shard_map(
        per_device, mesh=fine, in_specs=placed, out_specs=P(None, AXES, None), check_vma=False
    )
```

```python
import functools

import jax
import jax.numpy as jnp
from jax import lax
from jax.experimental import pallas as pl
from jax.experimental.pallas import tpu as pltpu
from jax.sharding import PartitionSpec as P

AXES = ("y", "x", "z", "c")
SIDE = 4


def routes(target):
    pairs = []
    for y in range(SIDE):
        for x in range(SIDE):
            for z in range(SIDE):
                for c in range(2):
                    ty, tx, tz, tc = target(y, x, z, c)
                    source = ((y * SIDE + x) * SIDE + z) * 2 + c
                    pairs.append((source, ((ty % SIDE * SIDE + tx % SIDE) * SIDE + tz % SIDE) * 2 + tc % 2))
    return pairs


def along_y(step):
    return routes(lambda y, x, z, c: (y + step, x, z, c))


def along_k(step):
    return routes(lambda y, x, z, c: (y, x, z + step, c) if c == 0 else (y, x + step, z, c))


def along_m(step):
    return routes(lambda y, x, z, c: (y, x + step, z, c) if c == 0 else (y, x, z + step, c))


OTHER_CORE = routes(lambda y, x, z, c: (y, x, z, c + 1))
VMEM_SPEC = pl.BlockSpec(memory_space=pltpu.VMEM)
SMEM_SPEC = pl.BlockSpec(memory_space=pltpu.SMEM)


def send(value, route):
    return lax.ppermute(value, AXES, route)


def contracted_split(rows, k_index):
    depth = rows.shape[1] // SIDE
    blocks = [lax.dynamic_slice_in_dim(rows, (k_index + s) % SIDE * depth, depth, axis=1) for s in range(SIDE)]
    moved = {s: send(blocks[s], along_k(s)) for s in (1, 3, 2)}
    return jnp.concatenate([blocks[0], moved[1], moved[2], moved[3]], axis=0)


def ring_gather(block, along):
    half = block.shape[0] // 2
    before = send(block, along(1))
    after = send(block, along(-1))
    return block, before, send(before[:half], along(1)), send(after[half:], along(-1)), after


def place_kernel(where_ref, own_ref, before_ref, far0_ref, far1_ref, after_ref, high_ref, low_ref):
    c, k_index, m_index = where_ref[0], where_ref[1], where_ref[2]
    wide = own_ref.shape[0] // SIDE
    half = wide // 2
    sources = [
        (own_ref, 0, 0, SIDE),
        (before_ref, 1, 0, SIDE),
        (far0_ref, 2, 0, SIDE // 2),
        (far1_ref, 2, SIDE // 2, SIDE // 2),
        (after_ref, 3, 0, SIDE),
    ]
    for ref, t, first, count in sources:
        m = (m_index - t + SIDE) % SIDE

        def body(i, carry, ref=ref, m=m, first=first):
            k = (k_index - i - first + SIDE) % SIDE
            row = jnp.where(c == 0, m * SIDE + k, k * SIDE + m) * wide
            front = ref[pl.ds(pl.multiple_of(i * wide + c * half, 8), half), :]
            back = ref[pl.ds(pl.multiple_of(i * wide + (1 - c) * half, 8), half), :]
            block = jnp.concatenate([front, back], axis=0)
            high = block.astype(jnp.bfloat16)
            low = (block - high.astype(jnp.float32)).astype(jnp.bfloat16)
            high_ref[pl.ds(pl.multiple_of(row, 16), wide), :] = high
            low_ref[pl.ds(pl.multiple_of(row, 16), wide), :] = low
            return carry

        lax.fori_loop(0, count, body, 0)


def place(where, blocks):
    depth = blocks[0].shape[1]
    total = blocks[0].shape[0] * SIDE
    size = total * depth
    return pl.pallas_call(
        place_kernel,
        out_shape=[jax.ShapeDtypeStruct((total, depth), jnp.bfloat16)] * 2,
        in_specs=[SMEM_SPEC] + [VMEM_SPEC] * 5,
        out_specs=[VMEM_SPEC] * 2,
        cost_estimate=pl.CostEstimate(flops=4 * size, bytes_accessed=8 * size, transcendentals=0),
        name="place",
    )(where, *blocks)


def product_kernel(spans, n_in, *refs):
    a_refs, (high_ref, low_ref), rest = refs[:n_in], refs[n_in : n_in + 2], refs[n_in + 2 :]
    out_refs, (a_ref,) = rest[:-1], rest[-1:]
    rows = a_ref.shape[0] // 2
    at = 0
    for source, first, count, _, _ in spans:
        value = a_refs[source][first : first + count, :]
        high = value.astype(jnp.bfloat16)
        a_ref[at : at + count, :] = high
        a_ref[rows + at : rows + at + count, :] = (value - high.astype(jnp.float32)).astype(jnp.bfloat16)
        at += count
    tile = 256
    dims = (((1,), (1,)), ((), ()))

    def body(j, carry):
        cols = pl.ds(pl.multiple_of(j * tile, tile), tile)
        both = lax.dot_general(a_ref[...], high_ref[cols, :], dims, preferred_element_type=jnp.float32)
        rest_of = lax.dot_general(a_ref[:rows, :], low_ref[cols, :], dims, preferred_element_type=jnp.float32)
        value = both[:rows] + (both[rows:] + rest_of)
        at = 0
        for _, _, count, out, out_first in spans:
            out_refs[out][out_first : out_first + count, cols] = value[at : at + count]
            at += count
        return carry

    lax.fori_loop(0, high_ref.shape[0] // tile, body, 0)


def product(sources, spans, out_rows, high, low, name):
    width, depth = high.shape
    rows = sum(span[2] for span in spans)
    return pl.pallas_call(
        functools.partial(product_kernel, spans, len(sources)),
        out_shape=[jax.ShapeDtypeStruct((count, width), jnp.float32) for count in out_rows],
        in_specs=[VMEM_SPEC] * (len(sources) + 2),
        out_specs=[VMEM_SPEC] * len(out_rows),
        scratch_shapes=[pltpu.VMEM((2 * rows, depth), jnp.bfloat16)],
        cost_estimate=pl.CostEstimate(
            flops=6 * rows * width * depth, bytes_accessed=4 * (rows * (width + depth) + width * depth), transcendentals=0
        ),
        name=name,
    )(*sources, high, low)


def span_list(tops, unit):
    spans, filled = [], [0] * 5
    for source, first, s_of in tops:
        for i, s in enumerate(s_of):
            if s == 2:
                for part, out in ((0, 3), (1, 4)):
                    spans.append((source, first + i * unit + part * unit // 2, unit // 2, out, filled[out]))
                    filled[out] += unit // 2
            else:
                out = {0: 0, 1: 1, 3: 2}[s]
                spans.append((source, first + i * unit, unit, out, filled[out]))
                filled[out] += unit
    return spans, filled


def ring_reduce(parts, halves):
    p0, p1, p3, front, back = parts
    low = send(front, along_k(-1))
    high = send(back, along_k(1))
    pick = halves
    p1 = p1 + jnp.concatenate(
        sum([[low[i * pick : (i + 1) * pick], jnp.zeros_like(low[:pick])] for i in range(low.shape[0] // pick)], []), axis=0
    )
    p3 = p3 + jnp.concatenate(
        sum([[jnp.zeros_like(high[:pick]), high[i * pick : (i + 1) * pick]] for i in range(high.shape[0] // pick)], []), axis=0
    )
    return p0 + send(p1, along_k(-1)) + send(p3, along_k(1))


def finish_kernel(where_ref, r0_ref, q1_ref, q2_ref, q3_ref, near_ref, far_ref, row_ref, col_ref, out_ref):
    c, y = where_ref[0], where_ref[3]
    half, width = q2_ref.shape[0] // 2, q2_ref.shape[1]
    for t, ref in enumerate((r0_ref, q1_ref, q2_ref, q3_ref)):
        cols = pl.ds(pl.multiple_of((y + t) % SIDE * width, 128), width)
        theirs = far_ref[...] if t == 2 else near_ref[{0: 0, 1: 1, 3: 2}[t]]
        for g, value in ((c, ref[:half, :]), (1 - c, theirs)):
            out_ref[g, :, cols] = value / (row_ref[g] + col_ref[g, :, cols])


def finish(where, r0, q1, q2, q3, near, far, row_gap, col_gap):
    half, width = far.shape
    size = 2 * half * SIDE * width
    return pl.pallas_call(
        finish_kernel,
        out_shape=jax.ShapeDtypeStruct((2, half, SIDE * width), jnp.float32),
        in_specs=[SMEM_SPEC] + [VMEM_SPEC] * 8,
        out_specs=VMEM_SPEC,
        cost_estimate=pl.CostEstimate(flops=3 * size, bytes_accessed=8 * size, transcendentals=0),
        name="finish",
    )(where, r0, q1, q2, q3, near, far, row_gap[:, :, None], col_gap[:, None, :])


def per_device(amplitudes, integrals, row_gap, col_gap):
    y, x, z, c = (lax.axis_index(name) for name in AXES)
    k_index = jnp.where(c == 0, z, x)
    m_index = jnp.where(c == 0, x, z)
    where = jnp.stack([c, k_index, m_index, y]).astype(jnp.int32)
    columns = jnp.swapaxes(integrals, 1, 2)

    def both_cores(value):
        own = lax.dynamic_index_in_dim(value, c, 0, keepdims=False)
        other = send(lax.dynamic_index_in_dim(value, 1 - c, 0, keepdims=False), OTHER_CORE)
        return jnp.concatenate([own, other], axis=0)

    rows = both_cores(amplitudes)
    cols = both_cores(columns)
    a_own, a_before, a_far0, a_far1, a_after = ring_gather(contracted_split(rows, k_index), along_y)
    high, low = place(where, ring_gather(contracted_split(cols, k_index), along_m))

    unit = rows.shape[0]
    spans, filled = span_list([(0, 0, range(SIDE))], unit)
    own = ring_reduce(product([a_own], spans, filled, high, low, "product_own"), unit // 2)
    spans, filled = span_list([(0, 0, range(SIDE)), (1, 0, range(SIDE))], unit)
    near = ring_reduce(product([a_before, a_after], spans, filled, high, low, "product_near"), unit // 2)
    spans, filled = span_list([(0, 0, (0, 1)), (1, 0, (2, 3))], unit)
    far = ring_reduce(product([a_far0, a_far1], spans, filled, high, low, "product_far"), unit // 2)

    q1 = send(near[:unit], along_y(-1))
    q3 = send(near[unit:], along_y(1))
    q2 = send(far, along_y(2))
    half = unit // 2
    near_theirs = send(jnp.stack([own[half:], q1[half:], q3[half:]]), OTHER_CORE)
    far_theirs = send(q2[half:], OTHER_CORE)
    return finish(where, own, q1, q2, q3, near_theirs, far_theirs, row_gap, col_gap)


def solution(mesh):
    fine = jax.sharding.Mesh(mesh.devices.reshape(SIDE, SIDE, SIDE, 2), AXES)
    placed = (P(None, AXES, None), P(None, None, AXES), P(None, AXES), P())
    return jax.shard_map(
        per_device, mesh=fine, in_specs=placed, out_specs=P(None, AXES, None), check_vma=False
    )
```

```python
import functools

import jax
import jax.numpy as jnp
from jax import lax
from jax.experimental import pallas as pl
from jax.experimental.pallas import tpu as pltpu
from jax.sharding import PartitionSpec as P

AXES = ("y", "x", "z", "c")
SIDE = 4


def routes(target):
    pairs = []
    for y in range(SIDE):
        for x in range(SIDE):
            for z in range(SIDE):
                for c in range(2):
                    ty, tx, tz, tc = target(y, x, z, c)
                    source = ((y * SIDE + x) * SIDE + z) * 2 + c
                    pairs.append((source, ((ty % SIDE * SIDE + tx % SIDE) * SIDE + tz % SIDE) * 2 + tc % 2))
    return pairs


def along_y(step):
    return routes(lambda y, x, z, c: (y + step, x, z, c))


def along_k(step):
    return routes(lambda y, x, z, c: (y, x, z + step, c) if c == 0 else (y, x + step, z, c))


def along_m(step):
    return routes(lambda y, x, z, c: (y, x + step, z, c) if c == 0 else (y, x, z + step, c))


OTHER_CORE = routes(lambda y, x, z, c: (y, x, z, c + 1))
VMEM_SPEC = pl.BlockSpec(memory_space=pltpu.VMEM)
SMEM_SPEC = pl.BlockSpec(memory_space=pltpu.SMEM)
GRANT = pltpu.CompilerParams(vmem_limit_bytes=20 * 2**20)


def send(value, route):
    return lax.ppermute(value, AXES, route)


def after(value, *earlier):
    return lax.optimization_barrier((value, *earlier))[0]


def ring_gather(block, along):
    half = block.shape[0] // 2
    low, high = send(block, along(1)), send(block, along(-1))
    return block, low, send(low[:half], along(1)), send(high[half:], along(-1)), high


def pack_kernel(where_ref, rows_ref, cols_ref, other_ref, *out_refs):
    c, k_index = where_ref[0], where_ref[1]
    tall, half, depth = rows_ref.shape[1], cols_ref.shape[1], out_refs[0].shape[1]
    for s, out_ref in enumerate(out_refs):
        span = pl.ds(pl.multiple_of((k_index + s) % SIDE * depth, 128), depth)
        out_ref[:tall, :] = rows_ref[c, :, span]
        out_ref[tall : 2 * tall, :] = other_ref[:tall, span]
        out_ref[pl.ds(pl.multiple_of(2 * tall + c * half, 8), half), :] = cols_ref[c, :, span]
        out_ref[pl.ds(pl.multiple_of(2 * tall + (1 - c) * half, 8), half), :] = other_ref[tall:, span]


def pack(where, rows, cols, other):
    height, depth = 2 * other.shape[0], other.shape[1] // SIDE
    return pl.pallas_call(
        pack_kernel,
        out_shape=[jax.ShapeDtypeStruct((height, depth), jnp.float32)] * SIDE,
        in_specs=[SMEM_SPEC] + [VMEM_SPEC] * 3,
        out_specs=[VMEM_SPEC] * SIDE,
        cost_estimate=pl.CostEstimate(flops=0, bytes_accessed=8 * height * depth * SIDE, transcendentals=0),
        compiler_params=GRANT,
        name="pack",
    )(where, rows, cols, other)


def place_kernel(sources, where_ref, *refs):
    refs, high_ref, low_ref = refs[: len(sources)], refs[-2], refs[-1]
    c, k_index, m_index = where_ref[0], where_ref[1], where_ref[2]
    for ref, (t, first, count) in zip(refs, sources):
        wide = ref.shape[0] // count
        m = (m_index - t + SIDE) % SIDE

        def body(i, carry, ref=ref, m=m, first=first):
            k = (k_index - i - first + SIDE) % SIDE
            row = jnp.where(c == 0, m * SIDE + k, k * SIDE + m) * wide
            block = ref[pl.ds(pl.multiple_of(i * wide, 8), wide), :]
            high = block.astype(jnp.bfloat16)
            low = (block - high.astype(jnp.float32)).astype(jnp.bfloat16)
            high_ref[pl.ds(pl.multiple_of(row, 16), wide), :] = high
            low_ref[pl.ds(pl.multiple_of(row, 16), wide), :] = low
            return carry

        lax.fori_loop(0, count, body, 0)


def place(where, blocks, sources, total, into=()):
    depth = blocks[0].shape[1]
    size = sum(block.shape[0] for block in blocks) * depth
    n = len(blocks)
    return pl.pallas_call(
        functools.partial(place_kernel, sources),
        out_shape=[jax.ShapeDtypeStruct((total, depth), jnp.bfloat16)] * 2,
        in_specs=[SMEM_SPEC] + [VMEM_SPEC] * (n + len(into)),
        out_specs=[VMEM_SPEC] * 2,
        input_output_aliases={n + 1 + i: i for i in range(len(into))},
        cost_estimate=pl.CostEstimate(flops=4 * size, bytes_accessed=8 * size, transcendentals=0),
        compiler_params=GRANT,
        name="place_far" if into else "place_near",
    )(where, *blocks, *into)


def product_kernel(spans, n_in, *refs):
    a_refs, (high_ref, low_ref), rest = refs[:n_in], refs[n_in : n_in + 2], refs[n_in + 2 :]
    out_refs, (a_ref,) = rest[:-1], rest[-1:]
    rows = a_ref.shape[0] // 2
    at = 0
    for source, first, count, _, _ in spans:
        value = a_refs[source][first : first + count, :]
        high = value.astype(jnp.bfloat16)
        a_ref[at : at + count, :] = high
        a_ref[rows + at : rows + at + count, :] = (value - high.astype(jnp.float32)).astype(jnp.bfloat16)
        at += count
    tile = 256
    dims = (((1,), (1,)), ((), ()))

    def body(j, carry):
        cols = pl.ds(pl.multiple_of(j * tile, tile), tile)
        both = lax.dot_general(a_ref[...], high_ref[cols, :], dims, preferred_element_type=jnp.float32)
        rest_of = lax.dot_general(a_ref[:rows, :], low_ref[cols, :], dims, preferred_element_type=jnp.float32)
        value = both[:rows] + (both[rows:] + rest_of)
        at = 0
        for _, _, count, out, out_first in spans:
            out_refs[out][out_first : out_first + count, cols] = value[at : at + count]
            at += count
        return carry

    lax.fori_loop(0, high_ref.shape[0] // tile, body, 0)


def product(sources, spans, out_rows, high, low, name):
    width, depth = high.shape
    rows = sum(span[2] for span in spans)
    return pl.pallas_call(
        functools.partial(product_kernel, spans, len(sources)),
        out_shape=[jax.ShapeDtypeStruct((count, width), jnp.float32) for count in out_rows],
        in_specs=[VMEM_SPEC] * (len(sources) + 2),
        out_specs=[VMEM_SPEC] * len(out_rows),
        scratch_shapes=[pltpu.VMEM((2 * rows, depth), jnp.bfloat16)],
        cost_estimate=pl.CostEstimate(
            flops=6 * rows * width * depth, bytes_accessed=4 * (rows * (width + depth) + width * depth), transcendentals=0
        ),
        compiler_params=GRANT,
        name=name,
    )(*sources, high, low)


def span_list(tops, unit):
    spans, filled = [], [0] * 5
    for source, first, s_of in tops:
        for i, s in enumerate(s_of):
            if s == 2:
                for part, out in ((0, 3), (1, 4)):
                    spans.append((source, first + i * unit + part * unit // 2, unit // 2, out, filled[out]))
                    filled[out] += unit // 2
            else:
                out = {0: 0, 1: 1, 3: 2}[s]
                spans.append((source, first + i * unit, unit, out, filled[out]))
                filled[out] += unit
    return spans, filled


def ring_reduce(parts, halves):
    p0, p1, p3, front, back = parts
    low = send(front, along_k(-1))
    high = send(back, along_k(1))
    pick = halves
    p1 = p1 + jnp.concatenate(
        sum([[low[i * pick : (i + 1) * pick], jnp.zeros_like(low[:pick])] for i in range(low.shape[0] // pick)], []), axis=0
    )
    p3 = p3 + jnp.concatenate(
        sum([[jnp.zeros_like(high[:pick]), high[i * pick : (i + 1) * pick]] for i in range(high.shape[0] // pick)], []), axis=0
    )
    return p0 + send(p1, along_k(-1)) + send(p3, along_k(1))


def direct_reduce(parts):
    p0, p1, p2, p3 = parts
    return p0 + send(p1, along_k(-1)) + send(p3, along_k(1)) + send(p2, along_k(2))


def finish_kernel(where_ref, r0_ref, q1_ref, q2_ref, q3_ref, near_ref, far_ref, row_ref, col_ref, out_ref):
    c, y = where_ref[0], where_ref[3]
    half, width = q2_ref.shape[0] // 2, q2_ref.shape[1]
    for t, ref in enumerate((r0_ref, q1_ref, q2_ref, q3_ref)):
        cols = pl.ds(pl.multiple_of((y + t) % SIDE * width, 128), width)
        theirs = far_ref[...] if t == 2 else near_ref[{0: 0, 1: 1, 3: 2}[t]]
        for g, value in ((c, ref[:half, :]), (1 - c, theirs)):
            out_ref[g, :, cols] = value / (row_ref[g] + col_ref[g, :, cols])


def finish(where, r0, q1, q2, q3, near, far, row_gap, col_gap):
    half, width = far.shape
    size = 2 * half * SIDE * width
    return pl.pallas_call(
        finish_kernel,
        out_shape=jax.ShapeDtypeStruct((2, half, SIDE * width), jnp.float32),
        in_specs=[SMEM_SPEC] + [VMEM_SPEC] * 8,
        out_specs=VMEM_SPEC,
        cost_estimate=pl.CostEstimate(flops=3 * size, bytes_accessed=8 * size, transcendentals=0),
        compiler_params=GRANT,
        name="finish",
    )(where, r0, q1, q2, q3, near, far, row_gap, col_gap)


def per_device(amplitudes, integrals, row_gap, col_gap):
    y, x, z, c = (lax.axis_index(name) for name in AXES)
    k_index = jnp.where(c == 0, z, x)
    m_index = jnp.where(c == 0, x, z)
    where = jnp.stack([c, k_index, m_index, y]).astype(jnp.int32)
    columns = jnp.swapaxes(integrals, 1, 2)

    tall = amplitudes.shape[1]
    other = send(jnp.concatenate([value[1 - c] for value in (amplitudes, columns)], axis=0), OTHER_CORE)
    packed = pack(where, amplitudes, columns, other)
    moved = [packed[0]] + [send(packed[s], along_k(s)) for s in (1, 2, 3)]
    a_block = jnp.concatenate([block[: 2 * tall] for block in moved], axis=0)
    b_block = jnp.concatenate([block[2 * tall :] for block in moved], axis=0)
    a_own, a_before, a_far0, a_far1, a_after = ring_gather(a_block, along_y)
    b_own, b_before, b_far0, b_far1, b_after = ring_gather(b_block, along_m)

    total = b_own.shape[0] * SIDE
    where, row_gap, col_gap = lax.optimization_barrier((where, row_gap[:, :, None], col_gap[:, None, :]))
    placed = place(where, [b_own, b_before, b_after], [(0, 0, 4), (1, 0, 4), (3, 0, 4)], total)
    high, low = place(where, [b_far0, b_far1], [(2, 0, 2), (2, 2, 2)], total, placed)

    unit = 2 * tall
    spans, filled = span_list([(0, 0, range(SIDE))], unit)
    own_parts = product([a_own], spans, filled, high, low, "product_own")
    own = ring_reduce(own_parts, unit // 2)
    spans, filled = span_list([(0, 0, range(SIDE)), (1, 0, range(SIDE))], unit)
    near_parts = product([after(a_before, own_parts[0]), a_after], spans, filled, high, low, "product_near")
    near = ring_reduce(near_parts, unit // 2)
    spans = [(s // 2, s % 2 * unit, unit, s, 0) for s in range(SIDE)]
    far = direct_reduce(product([after(a_far0, near_parts[0]), a_far1], spans, [unit] * SIDE, high, low, "product_far"))

    q1 = send(near[:unit], along_y(-1))
    q3 = send(near[unit:], along_y(1))
    q2 = send(far, along_y(2))
    half = unit // 2
    near_theirs = send(jnp.stack([own[half:], q1[half:], q3[half:]]), OTHER_CORE)
    far_theirs = send(q2[half:], OTHER_CORE)
    return finish(where, own, q1, q2, q3, near_theirs, far_theirs, row_gap, col_gap)


def solution(mesh):
    fine = jax.sharding.Mesh(mesh.devices.reshape(SIDE, SIDE, SIDE, 2), AXES)
    placed = (P(None, AXES, None), P(None, None, AXES), P(None, AXES), P())
    return jax.shard_map(
        per_device, mesh=fine, in_specs=placed, out_specs=P(None, AXES, None), check_vma=False
    )
```

```python
import functools

import jax
import jax.numpy as jnp
from jax import lax
from jax.experimental import pallas as pl
from jax.experimental.pallas import tpu as pltpu
from jax.sharding import PartitionSpec as P

AXES = ("y", "x", "z", "c")
SIDE = 4


def routes(target):
    pairs = []
    for y in range(SIDE):
        for x in range(SIDE):
            for z in range(SIDE):
                for c in range(2):
                    ty, tx, tz, tc = target(y, x, z, c)
                    source = ((y * SIDE + x) * SIDE + z) * 2 + c
                    pairs.append((source, ((ty % SIDE * SIDE + tx % SIDE) * SIDE + tz % SIDE) * 2 + tc % 2))
    return pairs


def along_y(step):
    return routes(lambda y, x, z, c: (y + step, x, z, c))


def along_k(step):
    return routes(lambda y, x, z, c: (y, x, z + step, c) if c == 0 else (y, x + step, z, c))


def along_m(step):
    return routes(lambda y, x, z, c: (y, x + step, z, c) if c == 0 else (y, x, z + step, c))


OTHER_CORE = routes(lambda y, x, z, c: (y, x, z, c + 1))
VMEM_SPEC = pl.BlockSpec(memory_space=pltpu.VMEM)
SMEM_SPEC = pl.BlockSpec(memory_space=pltpu.SMEM)
GRANT = pltpu.CompilerParams(vmem_limit_bytes=20 * 2**20)


def send(value, route):
    return lax.ppermute(value, AXES, route)


def after(value, *earlier):
    return lax.optimization_barrier((value, *earlier))[0]


def ring_near(block, along):
    return send(block, along(1)), send(block, along(-1))


def ring_far(low, high, along):
    half = low.shape[0] // 2
    return send(low[:half], along(1)), send(high[half:], along(-1))


def pack_kernel(where_ref, rows_ref, cols_ref, other_ref, *out_refs):
    c, k_index = where_ref[0], where_ref[1]
    tall, depth = rows_ref.shape[1], out_refs[0].shape[1]
    other_ref[:tall, :] = rows_ref[1 - c]
    other_ref[tall:, :] = cols_ref[1 - c]
    for s, out_ref in enumerate(out_refs):
        span = pl.ds(pl.multiple_of((k_index + s) % SIDE * depth, 128), depth)
        out_ref[:tall, :] = rows_ref[c, :, span]
        out_ref[tall:, :] = cols_ref[c, :, span]


def pack(where, rows, cols):
    height, depth = rows.shape[1] + cols.shape[1], rows.shape[2] // SIDE
    return pl.pallas_call(
        pack_kernel,
        out_shape=[jax.ShapeDtypeStruct((height, depth * SIDE), jnp.float32)]
        + [jax.ShapeDtypeStruct((height, depth), jnp.float32)] * SIDE,
        in_specs=[SMEM_SPEC] + [VMEM_SPEC] * 2,
        out_specs=[VMEM_SPEC] * (1 + SIDE),
        cost_estimate=pl.CostEstimate(flops=0, bytes_accessed=16 * height * depth * SIDE, transcendentals=0),
        compiler_params=GRANT,
        name="pack",
    )(where, rows, cols)


def split_kernel(where_ref, in_ref, *out_refs):
    k_index, depth = where_ref[1], out_refs[0].shape[1]
    for s, out_ref in enumerate(out_refs):
        out_ref[...] = in_ref[:, pl.ds(pl.multiple_of((k_index + s) % SIDE * depth, 128), depth)]


def split(where, value):
    height, depth = value.shape[0], value.shape[1] // SIDE
    return pl.pallas_call(
        split_kernel,
        out_shape=[jax.ShapeDtypeStruct((height, depth), jnp.float32)] * SIDE,
        in_specs=[SMEM_SPEC, VMEM_SPEC],
        out_specs=[VMEM_SPEC] * SIDE,
        cost_estimate=pl.CostEstimate(flops=0, bytes_accessed=8 * height * depth * SIDE, transcendentals=0),
        compiler_params=GRANT,
        name="split",
    )(where, value)


def join_kernel(own, tall, where_ref, *refs):
    c = where_ref[0]
    core = c if own else 1 - c
    a_ref, b_ref = refs[-2:]
    half = refs[0].shape[0] - tall
    for s, ref in enumerate(refs[:SIDE]):
        start = 2 * tall * s + (0 if own else tall)
        a_ref[start : start + tall, :] = ref[:tall, :]
        b_ref[pl.ds(pl.multiple_of(2 * half * s + core * half, 8), half), :] = ref[tall:, :]


def join(where, blocks, tall, into=()):
    height, depth = blocks[0].shape
    shapes = [(2 * tall * SIDE, depth), (2 * (height - tall) * SIDE, depth)]
    return pl.pallas_call(
        functools.partial(join_kernel, not into, tall),
        out_shape=[jax.ShapeDtypeStruct(shape, jnp.float32) for shape in shapes],
        in_specs=[SMEM_SPEC] + [VMEM_SPEC] * (SIDE + len(into)),
        out_specs=[VMEM_SPEC] * 2,
        input_output_aliases={SIDE + 1 + i: i for i in range(len(into))},
        cost_estimate=pl.CostEstimate(flops=0, bytes_accessed=8 * height * depth * SIDE, transcendentals=0),
        compiler_params=GRANT,
        name="join_other" if into else "join_own",
    )(where, *blocks, *into)


def place_kernel(sources, where_ref, *refs):
    refs, high_ref, low_ref = refs[: len(sources)], refs[-2], refs[-1]
    c, k_index, m_index = where_ref[0], where_ref[1], where_ref[2]
    for ref, (t, first, count) in zip(refs, sources):
        wide = ref.shape[0] // count
        m = (m_index - t + SIDE) % SIDE

        def body(i, carry, ref=ref, m=m, first=first):
            k = (k_index - i - first + SIDE) % SIDE
            row = jnp.where(c == 0, m * SIDE + k, k * SIDE + m) * wide
            block = ref[pl.ds(pl.multiple_of(i * wide, 8), wide), :]
            high = block.astype(jnp.bfloat16)
            low = (block - high.astype(jnp.float32)).astype(jnp.bfloat16)
            high_ref[pl.ds(pl.multiple_of(row, 16), wide), :] = high
            low_ref[pl.ds(pl.multiple_of(row, 16), wide), :] = low
            return carry

        lax.fori_loop(0, count, body, 0)


def place(where, blocks, sources, total, into=()):
    depth = blocks[0].shape[1]
    size = sum(block.shape[0] for block in blocks) * depth
    n = len(blocks)
    return pl.pallas_call(
        functools.partial(place_kernel, sources),
        out_shape=[jax.ShapeDtypeStruct((total, depth), jnp.bfloat16)] * 2,
        in_specs=[SMEM_SPEC] + [VMEM_SPEC] * (n + len(into)),
        out_specs=[VMEM_SPEC] * 2,
        input_output_aliases={n + 1 + i: i for i in range(len(into))},
        cost_estimate=pl.CostEstimate(flops=4 * size, bytes_accessed=8 * size, transcendentals=0),
        compiler_params=GRANT,
        name="place_far" if into else "place_near",
    )(where, *blocks, *into)


def product_kernel(spans, n_in, *refs):
    a_refs, (high_ref, low_ref), rest = refs[:n_in], refs[n_in : n_in + 2], refs[n_in + 2 :]
    out_refs, (a_ref,) = rest[:-1], rest[-1:]
    rows = a_ref.shape[0] // 2
    at = 0
    for source, first, count, _, _ in spans:
        value = a_refs[source][first : first + count, :]
        high = value.astype(jnp.bfloat16)
        a_ref[at : at + count, :] = high
        a_ref[rows + at : rows + at + count, :] = (value - high.astype(jnp.float32)).astype(jnp.bfloat16)
        at += count
    tile = 256
    dims = (((1,), (1,)), ((), ()))

    def body(j, carry):
        cols = pl.ds(pl.multiple_of(j * tile, tile), tile)
        both = lax.dot_general(a_ref[...], high_ref[cols, :], dims, preferred_element_type=jnp.float32)
        rest_of = lax.dot_general(a_ref[:rows, :], low_ref[cols, :], dims, preferred_element_type=jnp.float32)
        value = both[:rows] + (both[rows:] + rest_of)
        at = 0
        for _, _, count, out, out_first in spans:
            out_refs[out][out_first : out_first + count, cols] = value[at : at + count]
            at += count
        return carry

    lax.fori_loop(0, high_ref.shape[0] // tile, body, 0)


def product(sources, spans, out_rows, high, low, name):
    width, depth = high.shape
    rows = sum(span[2] for span in spans)
    return pl.pallas_call(
        functools.partial(product_kernel, spans, len(sources)),
        out_shape=[jax.ShapeDtypeStruct((count, width), jnp.float32) for count in out_rows],
        in_specs=[VMEM_SPEC] * (len(sources) + 2),
        out_specs=[VMEM_SPEC] * len(out_rows),
        scratch_shapes=[pltpu.VMEM((2 * rows, depth), jnp.bfloat16)],
        cost_estimate=pl.CostEstimate(
            flops=6 * rows * width * depth, bytes_accessed=4 * (rows * (width + depth) + width * depth), transcendentals=0
        ),
        compiler_params=GRANT,
        name=name,
    )(*sources, high, low)


def direct_reduce(parts):
    p0, p1, p2, p3 = parts
    return p0 + send(p1, along_k(-1)) + send(p3, along_k(1)) + send(p2, along_k(2))


def finish_kernel(where_ref, r0_ref, q1_ref, q2_ref, q3_ref, near_ref, last_ref, row_ref, col_ref, out_ref):
    c, y = where_ref[0], where_ref[3]
    half, width = q2_ref.shape[0] // 2, q2_ref.shape[1]
    for t, ref in enumerate((r0_ref, q1_ref, q2_ref, q3_ref)):
        cols = pl.ds(pl.multiple_of((y + t) % SIDE * width, 128), width)
        theirs = near_ref[t // 2] if t % 2 else last_ref[t // 2]
        for g, value in ((c, ref[:half, :]), (1 - c, theirs)):
            out_ref[g, :, cols] = value / (row_ref[g] + col_ref[g, :, cols])


def finish(where, r0, q1, q2, q3, near, last, row_gap, col_gap):
    _, half, width = last.shape
    size = 2 * half * SIDE * width
    return pl.pallas_call(
        finish_kernel,
        out_shape=jax.ShapeDtypeStruct((2, half, SIDE * width), jnp.float32),
        in_specs=[SMEM_SPEC] + [VMEM_SPEC] * 8,
        out_specs=VMEM_SPEC,
        cost_estimate=pl.CostEstimate(flops=3 * size, bytes_accessed=8 * size, transcendentals=0),
        compiler_params=GRANT,
        name="finish",
    )(where, r0, q1, q2, q3, near, last, row_gap, col_gap)


def per_device(amplitudes, integrals, row_gap, col_gap):
    y, x, z, c = (lax.axis_index(name) for name in AXES)
    k_index = jnp.where(c == 0, z, x)
    m_index = jnp.where(c == 0, x, z)
    where = jnp.stack([c, k_index, m_index, y]).astype(jnp.int32)
    columns = jnp.swapaxes(integrals, 1, 2)

    tall = amplitudes.shape[1]
    other, *packed = pack(where, amplitudes, columns)
    other_packed = split(where, send(other, OTHER_CORE))
    own_moved, other_moved = (
        [blocks[0]] + [send(blocks[s], along_k(s)) for s in (1, 2, 3)] for blocks in (packed, other_packed)
    )
    a_own, b_own = join(where, other_moved, tall, join(where, own_moved, tall))

    a_near = ring_near(a_own, along_y)
    b_near = ring_near(b_own, along_m)
    b_far = ring_far(*b_near, along_m)
    total = b_own.shape[0] * SIDE
    where, row_gap, col_gap = lax.optimization_barrier((where, row_gap[:, :, None], col_gap[:, None, :]))
    placed = place(where, [b_own, *b_near], [(0, 0, 4), (1, 0, 4), (3, 0, 4)], total)
    a_near, placed = lax.optimization_barrier((a_near, placed))
    a_far = ring_far(*a_near, along_y)
    high, low = place(where, b_far, [(2, 0, 2), (2, 2, 2)], total, placed)

    unit = 2 * tall
    spans = [(t, s * unit, unit, s, t * unit) for t in range(2) for s in range(SIDE)]
    near_parts = product(a_near, spans, [2 * unit] * SIDE, high, low, "product_near")
    near = direct_reduce(near_parts)
    q1 = send(near[:unit], along_y(-1))
    q3 = send(near[unit:], along_y(1))
    spans = [(s // 2, s % 2 * unit, unit, s, 0) for s in range(SIDE)]
    far_parts = product([after(a_far[0], near_parts[0]), a_far[1]], spans, [unit] * SIDE, high, low, "product_far")
    far = direct_reduce([after(far_parts[0], near), *far_parts[1:]])
    q2 = send(far, along_y(2))
    spans = [(0, s * unit, unit, s, 0) for s in range(SIDE)]
    own_parts = product([after(a_own, far_parts[0])], spans, [unit] * SIDE, high, low, "product_own")
    own_parts = [after(own_parts[0], far, q1, q3)] + [after(part, near) for part in own_parts[1:]]
    own = direct_reduce(own_parts)

    near_theirs = send(jnp.stack([q1[tall:], q3[tall:]]), OTHER_CORE)
    last_theirs = send(jnp.stack([own[tall:], q2[tall:]]), OTHER_CORE)
    return finish(where, own, q1, q2, q3, near_theirs, last_theirs, row_gap, col_gap)


def solution(mesh):
    fine = jax.sharding.Mesh(mesh.devices.reshape(SIDE, SIDE, SIDE, 2), AXES)
    placed = (P(None, AXES, None), P(None, None, AXES), P(None, AXES), P())
    return jax.shard_map(
        per_device, mesh=fine, in_specs=placed, out_specs=P(None, AXES, None), check_vma=False
    )
```

```python
import functools

import jax
import jax.numpy as jnp
from jax import lax
from jax.experimental import pallas as pl
from jax.experimental.pallas import tpu as pltpu
from jax.sharding import PartitionSpec as P

AXES = ("y", "x", "z", "c")
SIDE = 4


def routes(target):
    pairs = []
    for y in range(SIDE):
        for x in range(SIDE):
            for z in range(SIDE):
                for c in range(2):
                    ty, tx, tz, tc = target(y, x, z, c)
                    source = ((y * SIDE + x) * SIDE + z) * 2 + c
                    pairs.append((source, ((ty % SIDE * SIDE + tx % SIDE) * SIDE + tz % SIDE) * 2 + tc % 2))
    return pairs


def along_y(step):
    return routes(lambda y, x, z, c: (y + step, x, z, c))


def along_k(step):
    return routes(lambda y, x, z, c: (y, x, z + step, c) if c == 0 else (y, x + step, z, c))


def along_m(step):
    return routes(lambda y, x, z, c: (y, x + step, z, c) if c == 0 else (y, x, z + step, c))


OTHER_CORE = routes(lambda y, x, z, c: (y, x, z, c + 1))
VMEM_SPEC = pl.BlockSpec(memory_space=pltpu.VMEM)
SMEM_SPEC = pl.BlockSpec(memory_space=pltpu.SMEM)
GRANT = pltpu.CompilerParams(vmem_limit_bytes=20 * 2**20)


def send(value, route):
    return lax.ppermute(value, AXES, route)


def after(value, *earlier):
    return lax.optimization_barrier((value, *earlier))[0]


def ring_near(block, along):
    return send(block, along(1)), send(block, along(-1))


def ring_far(low, high, along):
    half = low.shape[0] // 2
    return send(low[:half], along(1)), send(high[half:], along(-1))


def pack_kernel(where_ref, rows_ref, cols_ref, other_ref, *out_refs):
    c, k_index = where_ref[0], where_ref[1]
    tall, depth = rows_ref.shape[1], out_refs[0].shape[1]
    other_ref[:tall, :] = rows_ref[1 - c]
    other_ref[tall:, :] = cols_ref[1 - c]
    for s, out_ref in enumerate(out_refs):
        span = pl.ds(pl.multiple_of((k_index + s) % SIDE * depth, 128), depth)
        out_ref[:tall, :] = rows_ref[c, :, span]
        out_ref[tall:, :] = cols_ref[c, :, span]


def pack(where, rows, cols):
    height, depth = rows.shape[1] + cols.shape[1], rows.shape[2] // SIDE
    return pl.pallas_call(
        pack_kernel,
        out_shape=[jax.ShapeDtypeStruct((height, depth * SIDE), jnp.float32)]
        + [jax.ShapeDtypeStruct((height, depth), jnp.float32)] * SIDE,
        in_specs=[SMEM_SPEC] + [VMEM_SPEC] * 2,
        out_specs=[VMEM_SPEC] * (1 + SIDE),
        cost_estimate=pl.CostEstimate(flops=0, bytes_accessed=16 * height * depth * SIDE, transcendentals=0),
        compiler_params=GRANT,
        name="pack",
    )(where, rows, cols)


def split_kernel(where_ref, in_ref, *out_refs):
    k_index, depth = where_ref[1], out_refs[0].shape[1]
    for s, out_ref in enumerate(out_refs):
        out_ref[...] = in_ref[:, pl.ds(pl.multiple_of((k_index + s) % SIDE * depth, 128), depth)]


def split(where, value):
    height, depth = value.shape[0], value.shape[1] // SIDE
    return pl.pallas_call(
        split_kernel,
        out_shape=[jax.ShapeDtypeStruct((height, depth), jnp.float32)] * SIDE,
        in_specs=[SMEM_SPEC, VMEM_SPEC],
        out_specs=[VMEM_SPEC] * SIDE,
        cost_estimate=pl.CostEstimate(flops=0, bytes_accessed=8 * height * depth * SIDE, transcendentals=0),
        compiler_params=GRANT,
        name="split",
    )(where, value)


def join_kernel(own, tall, where_ref, *refs):
    c = where_ref[0]
    core = c if own else 1 - c
    a_ref, b_ref = refs[-2:]
    half = refs[0].shape[0] - tall
    for s, ref in enumerate(refs[:SIDE]):
        start = 2 * tall * s + (0 if own else tall)
        a_ref[start : start + tall, :] = ref[:tall, :]
        b_ref[pl.ds(pl.multiple_of(2 * half * s + core * half, 8), half), :] = ref[tall:, :]


def join(where, blocks, tall, into=()):
    height, depth = blocks[0].shape
    shapes = [(2 * tall * SIDE, depth), (2 * (height - tall) * SIDE, depth)]
    return pl.pallas_call(
        functools.partial(join_kernel, not into, tall),
        out_shape=[jax.ShapeDtypeStruct(shape, jnp.float32) for shape in shapes],
        in_specs=[SMEM_SPEC] + [VMEM_SPEC] * (SIDE + len(into)),
        out_specs=[VMEM_SPEC] * 2,
        input_output_aliases={SIDE + 1 + i: i for i in range(len(into))},
        cost_estimate=pl.CostEstimate(flops=0, bytes_accessed=8 * height * depth * SIDE, transcendentals=0),
        compiler_params=GRANT,
        name="join_other" if into else "join_own",
    )(where, *blocks, *into)


def place_kernel(sources, where_ref, *refs):
    refs, high_ref, low_ref = refs[: len(sources)], refs[-2], refs[-1]
    c, k_index, m_index = where_ref[0], where_ref[1], where_ref[2]
    for ref, (t, first, count) in zip(refs, sources):
        wide = ref.shape[0] // count
        m = (m_index - t + SIDE) % SIDE

        def body(i, carry, ref=ref, m=m, first=first):
            k = (k_index - i - first + SIDE) % SIDE
            row = jnp.where(c == 0, m * SIDE + k, k * SIDE + m) * wide
            block = ref[pl.ds(pl.multiple_of(i * wide, 8), wide), :]
            high = block.astype(jnp.bfloat16)
            low = (block - high.astype(jnp.float32)).astype(jnp.bfloat16)
            high_ref[pl.ds(pl.multiple_of(row, 16), wide), :] = high
            low_ref[pl.ds(pl.multiple_of(row, 16), wide), :] = low
            return carry

        lax.fori_loop(0, count, body, 0)


def place(where, blocks, sources, total, into=()):
    depth = blocks[0].shape[1]
    size = sum(block.shape[0] for block in blocks) * depth
    n = len(blocks)
    return pl.pallas_call(
        functools.partial(place_kernel, sources),
        out_shape=[jax.ShapeDtypeStruct((total, depth), jnp.bfloat16)] * 2,
        in_specs=[SMEM_SPEC] + [VMEM_SPEC] * (n + len(into)),
        out_specs=[VMEM_SPEC] * 2,
        input_output_aliases={n + 1 + i: i for i in range(len(into))},
        cost_estimate=pl.CostEstimate(flops=4 * size, bytes_accessed=8 * size, transcendentals=0),
        compiler_params=GRANT,
        name="place_far" if into else "place_near",
    )(where, *blocks, *into)


def product_kernel(spans, n_in, *refs):
    a_refs, (high_ref, low_ref), rest = refs[:n_in], refs[n_in : n_in + 2], refs[n_in + 2 :]
    out_refs, (a_ref,) = rest[:-1], rest[-1:]
    rows = a_ref.shape[0] // 2
    at = 0
    for source, first, count, _, _ in spans:
        value = a_refs[source][first : first + count, :]
        high = value.astype(jnp.bfloat16)
        a_ref[at : at + count, :] = high
        a_ref[rows + at : rows + at + count, :] = (value - high.astype(jnp.float32)).astype(jnp.bfloat16)
        at += count
    tile = 256
    dims = (((1,), (1,)), ((), ()))

    def body(j, carry):
        cols = pl.ds(pl.multiple_of(j * tile, tile), tile)
        both = lax.dot_general(a_ref[...], high_ref[cols, :], dims, preferred_element_type=jnp.float32)
        rest_of = lax.dot_general(a_ref[:rows, :], low_ref[cols, :], dims, preferred_element_type=jnp.float32)
        value = both[:rows] + (both[rows:] + rest_of)
        at = 0
        for _, _, count, out, out_first in spans:
            out_refs[out][out_first : out_first + count, cols] = value[at : at + count]
            at += count
        return carry

    lax.fori_loop(0, high_ref.shape[0] // tile, body, 0)


def product(sources, spans, out_rows, high, low, name):
    width, depth = high.shape
    rows = sum(span[2] for span in spans)
    return pl.pallas_call(
        functools.partial(product_kernel, spans, len(sources)),
        out_shape=[jax.ShapeDtypeStruct((count, width), jnp.float32) for count in out_rows],
        in_specs=[VMEM_SPEC] * (len(sources) + 2),
        out_specs=[VMEM_SPEC] * len(out_rows),
        scratch_shapes=[pltpu.VMEM((2 * rows, depth), jnp.bfloat16)],
        cost_estimate=pl.CostEstimate(
            flops=6 * rows * width * depth, bytes_accessed=4 * (rows * (width + depth) + width * depth), transcendentals=0
        ),
        compiler_params=GRANT,
        name=name,
    )(*sources, high, low)


def direct_reduce(parts):
    p0, p1, p2, p3 = parts
    return p0 + send(p1, along_k(-1)) + send(p3, along_k(1)) + send(p2, along_k(2))


def finish_kernel(turns, where_ref, *refs):
    mine_refs, (theirs_ref, row_ref, col_ref) = refs[:2], refs[2:5]
    out_ref, value_ref, sems = refs[-3:]
    c, y = where_ref[0], where_ref[3]
    half, width = theirs_ref.shape[1:]
    copies = []
    for i, t in enumerate(turns):
        cols = pl.ds(pl.multiple_of((y + t) % SIDE * width, 128), width)
        for j, (g, value) in enumerate(((c, mine_refs[i][:half, :]), (1 - c, theirs_ref[i]))):
            value_ref[i, j] = value / (row_ref[g] + col_ref[g, :, cols])
            copies.append(pltpu.make_async_copy(value_ref.at[i, j], out_ref.at[g, :, cols], sems.at[i, j]))
            copies[-1].start()
    for copy in copies:
        copy.wait()


def finish(where, mine, theirs, row_gap, col_gap, turns, into=()):
    _, half, width = theirs.shape
    size = 4 * half * width
    return pl.pallas_call(
        functools.partial(finish_kernel, turns),
        out_shape=jax.ShapeDtypeStruct((2, half, SIDE * width), jnp.float32),
        in_specs=[SMEM_SPEC] + [VMEM_SPEC] * 5 + [pl.BlockSpec(memory_space=pl.ANY)] * len(into),
        out_specs=pl.BlockSpec(memory_space=pl.ANY),
        scratch_shapes=[pltpu.VMEM((2, 2, half, width), jnp.float32), pltpu.SemaphoreType.DMA((2, 2))],
        input_output_aliases={6: 0} if into else {},
        cost_estimate=pl.CostEstimate(flops=3 * size, bytes_accessed=8 * size, transcendentals=0),
        compiler_params=GRANT,
        name="finish_last" if into else "finish_near",
    )(where, *mine, theirs, row_gap, col_gap, *into)


def per_device(amplitudes, integrals, row_gap, col_gap):
    y, x, z, c = (lax.axis_index(name) for name in AXES)
    k_index = jnp.where(c == 0, z, x)
    m_index = jnp.where(c == 0, x, z)
    where = jnp.stack([c, k_index, m_index, y]).astype(jnp.int32)
    columns = jnp.swapaxes(integrals, 1, 2)

    tall = amplitudes.shape[1]
    other, *packed = pack(where, amplitudes, columns)
    other_packed = split(where, send(other, OTHER_CORE))
    own_moved, other_moved = (
        [blocks[0]] + [send(blocks[s], along_k(s)) for s in (1, 2, 3)] for blocks in (packed, other_packed)
    )
    a_own, b_own = join(where, other_moved, tall, join(where, own_moved, tall))

    a_near = ring_near(a_own, along_y)
    b_near = ring_near(b_own, along_m)
    b_far = ring_far(*b_near, along_m)
    total = b_own.shape[0] * SIDE
    where, row_gap, col_gap = lax.optimization_barrier((where, row_gap[:, :, None], col_gap[:, None, :]))
    placed = place(where, [b_own, *b_near], [(0, 0, 4), (1, 0, 4), (3, 0, 4)], total)
    a_near, placed = lax.optimization_barrier((a_near, placed))
    a_far = ring_far(*a_near, along_y)
    high, low = place(where, b_far, [(2, 0, 2), (2, 2, 2)], total, placed)

    unit = 2 * tall
    spans = [(t, s * unit, unit, s, t * unit) for t in range(2) for s in range(SIDE)]
    near_parts = product(a_near, spans, [2 * unit] * SIDE, high, low, "product_near")
    near = direct_reduce(near_parts)
    q1 = send(near[:unit], along_y(-1))
    q3 = send(near[unit:], along_y(1))
    spans = [(s // 2, s % 2 * unit, unit, s, 0) for s in range(SIDE)]
    far_parts = product([after(a_far[0], near_parts[0]), a_far[1]], spans, [unit] * SIDE, high, low, "product_far")
    far = direct_reduce([after(far_parts[0], near), *far_parts[1:]])
    q2 = send(far, along_y(2))
    spans = [(0, s * unit, unit, s, 0) for s in range(SIDE)]
    own_parts = product([after(a_own, far_parts[0])], spans, [unit] * SIDE, high, low, "product_own")
    near_theirs = send(jnp.stack([q1[tall:], q3[tall:]]), OTHER_CORE)
    done = finish(where, [q1, q3], near_theirs, row_gap, col_gap, (1, 3))
    own_parts = [after(own_parts[0], far, near_theirs)] + [after(part, near) for part in own_parts[1:]]
    own = direct_reduce(own_parts)

    last_theirs = send(jnp.stack([own[tall:], q2[tall:]]), OTHER_CORE)
    return finish(where, [own, q2], last_theirs, row_gap, col_gap, (0, 2), (done,))


def solution(mesh):
    fine = jax.sharding.Mesh(mesh.devices.reshape(SIDE, SIDE, SIDE, 2), AXES)
    placed = (P(None, AXES, None), P(None, None, AXES), P(None, AXES), P())
    return jax.shard_map(
        per_device, mesh=fine, in_specs=placed, out_specs=P(None, AXES, None), check_vma=False
    )
```

```python
import functools

import jax
import jax.numpy as jnp
from jax import lax
from jax.experimental import pallas as pl
from jax.experimental.pallas import tpu as pltpu
from jax.sharding import PartitionSpec as P

AXES = ("y", "x", "z", "c")
SIDE = 4


def routes(target):
    pairs = []
    for y in range(SIDE):
        for x in range(SIDE):
            for z in range(SIDE):
                for c in range(2):
                    ty, tx, tz, tc = target(y, x, z, c)
                    source = ((y * SIDE + x) * SIDE + z) * 2 + c
                    pairs.append((source, ((ty % SIDE * SIDE + tx % SIDE) * SIDE + tz % SIDE) * 2 + tc % 2))
    return pairs


def along_y(step):
    return routes(lambda y, x, z, c: (y + step, x, z, c))


def along_k(step):
    return routes(lambda y, x, z, c: (y, x, z + step, c) if c == 0 else (y, x + step, z, c))


def along_m(step):
    return routes(lambda y, x, z, c: (y, x + step, z, c) if c == 0 else (y, x, z + step, c))


OTHER_CORE = routes(lambda y, x, z, c: (y, x, z, c + 1))
VMEM_SPEC = pl.BlockSpec(memory_space=pltpu.VMEM)
SMEM_SPEC = pl.BlockSpec(memory_space=pltpu.SMEM)
GRANT = pltpu.CompilerParams(vmem_limit_bytes=20 * 2**20)


def send(value, route):
    return lax.ppermute(value, AXES, route)


def after(value, *earlier):
    return lax.optimization_barrier((value, *earlier))[0]


def ring_near(block, along):
    return send(block, along(1)), send(block, along(-1))


def ring_far(low, high, along):
    half = low.shape[0] // 2
    return send(low[:half], along(1)), send(high[half:], along(-1))


def pack_kernel(where_ref, rows_ref, cols_ref, other_ref, *out_refs):
    c, k_index = where_ref[0], where_ref[1]
    tall, depth = rows_ref.shape[1], out_refs[0].shape[1]
    other_ref[:tall, :] = rows_ref[1 - c]
    other_ref[tall:, :] = cols_ref[1 - c]
    for s, out_ref in enumerate(out_refs):
        span = pl.ds(pl.multiple_of((k_index + s) % SIDE * depth, 128), depth)
        out_ref[:tall, :] = rows_ref[c, :, span]
        out_ref[tall:, :] = cols_ref[c, :, span]


def pack(where, rows, cols):
    height, depth = rows.shape[1] + cols.shape[1], rows.shape[2] // SIDE
    return pl.pallas_call(
        pack_kernel,
        out_shape=[jax.ShapeDtypeStruct((height, depth * SIDE), jnp.float32)]
        + [jax.ShapeDtypeStruct((height, depth), jnp.float32)] * SIDE,
        in_specs=[SMEM_SPEC] + [VMEM_SPEC] * 2,
        out_specs=[VMEM_SPEC] * (1 + SIDE),
        cost_estimate=pl.CostEstimate(flops=0, bytes_accessed=16 * height * depth * SIDE, transcendentals=0),
        compiler_params=GRANT,
        name="pack",
    )(where, rows, cols)


def split_kernel(where_ref, in_ref, *out_refs):
    k_index, depth = where_ref[1], out_refs[0].shape[1]
    for s, out_ref in enumerate(out_refs):
        out_ref[...] = in_ref[:, pl.ds(pl.multiple_of((k_index + s) % SIDE * depth, 128), depth)]


def split(where, value):
    height, depth = value.shape[0], value.shape[1] // SIDE
    return pl.pallas_call(
        split_kernel,
        out_shape=[jax.ShapeDtypeStruct((height, depth), jnp.float32)] * SIDE,
        in_specs=[SMEM_SPEC, VMEM_SPEC],
        out_specs=[VMEM_SPEC] * SIDE,
        cost_estimate=pl.CostEstimate(flops=0, bytes_accessed=8 * height * depth * SIDE, transcendentals=0),
        compiler_params=GRANT,
        name="split",
    )(where, value)


def join_kernel(own, tall, where_ref, *refs):
    c = where_ref[0]
    core = c if own else 1 - c
    a_ref, b_ref = refs[-2:]
    half = refs[0].shape[0] - tall
    for s, ref in enumerate(refs[:SIDE]):
        start = 2 * tall * s + (0 if own else tall)
        a_ref[start : start + tall, :] = ref[:tall, :]
        b_ref[pl.ds(pl.multiple_of(2 * half * s + core * half, 8), half), :] = ref[tall:, :]


def join(where, blocks, tall, into=()):
    height, depth = blocks[0].shape
    shapes = [(2 * tall * SIDE, depth), (2 * (height - tall) * SIDE, depth)]
    return pl.pallas_call(
        functools.partial(join_kernel, not into, tall),
        out_shape=[jax.ShapeDtypeStruct(shape, jnp.float32) for shape in shapes],
        in_specs=[SMEM_SPEC] + [VMEM_SPEC] * (SIDE + len(into)),
        out_specs=[VMEM_SPEC] * 2,
        input_output_aliases={SIDE + 1 + i: i for i in range(len(into))},
        cost_estimate=pl.CostEstimate(flops=0, bytes_accessed=8 * height * depth * SIDE, transcendentals=0),
        compiler_params=GRANT,
        name="join_other" if into else "join_own",
    )(where, *blocks, *into)


def place_kernel(sources, where_ref, *refs):
    refs, high_ref, low_ref = refs[: len(sources)], refs[-2], refs[-1]
    c, k_index, m_index = where_ref[0], where_ref[1], where_ref[2]
    for ref, (t, first, count) in zip(refs, sources):
        wide = ref.shape[0] // count
        m = (m_index - t + SIDE) % SIDE

        def body(i, carry, ref=ref, m=m, first=first):
            k = (k_index - i - first + SIDE) % SIDE
            row = jnp.where(c == 0, m * SIDE + k, k * SIDE + m) * wide
            block = ref[pl.ds(pl.multiple_of(i * wide, 8), wide), :]
            high = block.astype(jnp.bfloat16)
            low = (block - high.astype(jnp.float32)).astype(jnp.bfloat16)
            high_ref[pl.ds(pl.multiple_of(row, 16), wide), :] = high
            low_ref[pl.ds(pl.multiple_of(row, 16), wide), :] = low
            return carry

        lax.fori_loop(0, count, body, 0)


def place(where, blocks, sources, total, into=()):
    depth = blocks[0].shape[1]
    size = sum(block.shape[0] for block in blocks) * depth
    n = len(blocks)
    return pl.pallas_call(
        functools.partial(place_kernel, sources),
        out_shape=[jax.ShapeDtypeStruct((total, depth), jnp.bfloat16)] * 2,
        in_specs=[SMEM_SPEC] + [VMEM_SPEC] * (n + len(into)),
        out_specs=[VMEM_SPEC] * 2,
        input_output_aliases={n + 1 + i: i for i in range(len(into))},
        cost_estimate=pl.CostEstimate(flops=4 * size, bytes_accessed=8 * size, transcendentals=0),
        compiler_params=GRANT,
        name="place_far" if into else "place_near",
    )(where, *blocks, *into)


def product_kernel(spans, n_in, *refs):
    a_refs, (high_ref, low_ref), rest = refs[:n_in], refs[n_in : n_in + 2], refs[n_in + 2 :]
    out_refs, (a_ref,) = rest[:-1], rest[-1:]
    rows = a_ref.shape[0] // 2
    at = 0
    for source, first, count, _, _ in spans:
        value = a_refs[source][first : first + count, :]
        high = value.astype(jnp.bfloat16)
        a_ref[at : at + count, :] = high
        a_ref[rows + at : rows + at + count, :] = (value - high.astype(jnp.float32)).astype(jnp.bfloat16)
        at += count
    tile = 256
    dims = (((1,), (1,)), ((), ()))

    def body(j, carry):
        cols = pl.ds(pl.multiple_of(j * tile, tile), tile)
        both = lax.dot_general(a_ref[...], high_ref[cols, :], dims, preferred_element_type=jnp.float32)
        rest_of = lax.dot_general(a_ref[:rows, :], low_ref[cols, :], dims, preferred_element_type=jnp.float32)
        value = both[:rows] + (both[rows:] + rest_of)
        at = 0
        for _, _, count, out, out_first in spans:
            out_refs[out][out_first : out_first + count, cols] = value[at : at + count]
            at += count
        return carry

    lax.fori_loop(0, high_ref.shape[0] // tile, body, 0, unroll=True)


def product(sources, spans, out_rows, high, low, name):
    width, depth = high.shape
    rows = sum(span[2] for span in spans)
    return pl.pallas_call(
        functools.partial(product_kernel, spans, len(sources)),
        out_shape=[jax.ShapeDtypeStruct((count, width), jnp.float32) for count in out_rows],
        in_specs=[VMEM_SPEC] * (len(sources) + 2),
        out_specs=[VMEM_SPEC] * len(out_rows),
        scratch_shapes=[pltpu.VMEM((2 * rows, depth), jnp.bfloat16)],
        cost_estimate=pl.CostEstimate(
            flops=6 * rows * width * depth, bytes_accessed=4 * (rows * (width + depth) + width * depth), transcendentals=0
        ),
        compiler_params=GRANT,
        name=name,
    )(*sources, high, low)


def direct_reduce(parts):
    p0, p1, p2, p3 = parts
    return p0 + send(p1, along_k(-1)) + send(p3, along_k(1)) + send(p2, along_k(2))


def finish_kernel(turns, where_ref, *refs):
    mine_refs, (theirs_ref, row_ref, col_ref) = refs[:2], refs[2:5]
    out_ref, value_ref, sems = refs[-3:]
    c, y = where_ref[0], where_ref[3]
    half, width = theirs_ref.shape[1:]
    copies = []
    for i, t in enumerate(turns):
        cols = pl.ds(pl.multiple_of((y + t) % SIDE * width, 128), width)
        for j, (g, value) in enumerate(((c, mine_refs[i][:half, :]), (1 - c, theirs_ref[i]))):
            value_ref[i, j] = value / (row_ref[g] + col_ref[g, :, cols])
            copies.append(pltpu.make_async_copy(value_ref.at[i, j], out_ref.at[g, :, cols], sems.at[i, j]))
            copies[-1].start()
    for copy in copies:
        copy.wait()


def finish(where, mine, theirs, row_gap, col_gap, turns, into=()):
    _, half, width = theirs.shape
    size = 4 * half * width
    return pl.pallas_call(
        functools.partial(finish_kernel, turns),
        out_shape=jax.ShapeDtypeStruct((2, half, SIDE * width), jnp.float32),
        in_specs=[SMEM_SPEC] + [VMEM_SPEC] * 5 + [pl.BlockSpec(memory_space=pl.ANY)] * len(into),
        out_specs=pl.BlockSpec(memory_space=pl.ANY),
        scratch_shapes=[pltpu.VMEM((2, 2, half, width), jnp.float32), pltpu.SemaphoreType.DMA((2, 2))],
        input_output_aliases={6: 0} if into else {},
        cost_estimate=pl.CostEstimate(flops=3 * size, bytes_accessed=8 * size, transcendentals=0),
        compiler_params=GRANT,
        name="finish_last" if into else "finish_near",
    )(where, *mine, theirs, row_gap, col_gap, *into)


def per_device(amplitudes, integrals, row_gap, col_gap):
    y, x, z, c = (lax.axis_index(name) for name in AXES)
    k_index = jnp.where(c == 0, z, x)
    m_index = jnp.where(c == 0, x, z)
    where = jnp.stack([c, k_index, m_index, y]).astype(jnp.int32)
    columns = jnp.swapaxes(integrals, 1, 2)

    tall = amplitudes.shape[1]
    other, *packed = pack(where, amplitudes, columns)
    other_packed = split(where, send(other, OTHER_CORE))
    own_moved, other_moved = (
        [blocks[0]] + [send(blocks[s], along_k(s)) for s in (1, 2, 3)] for blocks in (packed, other_packed)
    )
    a_own, b_own = join(where, other_moved, tall, join(where, own_moved, tall))

    a_near = ring_near(a_own, along_y)
    b_near = ring_near(b_own, along_m)
    b_far = ring_far(*b_near, along_m)
    total = b_own.shape[0] * SIDE
    where, row_gap, col_gap = lax.optimization_barrier((where, row_gap[:, :, None], col_gap[:, None, :]))
    placed = place(where, [b_own, *b_near], [(0, 0, 4), (1, 0, 4), (3, 0, 4)], total)
    a_near, placed = lax.optimization_barrier((a_near, placed))
    a_far = ring_far(*a_near, along_y)
    high, low = place(where, b_far, [(2, 0, 2), (2, 2, 2)], total, placed)

    unit = 2 * tall
    spans = [(t, s * unit, unit, s, t * unit) for t in range(2) for s in range(SIDE)]
    near_parts = product(a_near, spans, [2 * unit] * SIDE, high, low, "product_near")
    near = direct_reduce(near_parts)
    q1 = send(near[:unit], along_y(-1))
    q3 = send(near[unit:], along_y(1))
    spans = [(s // 2, s % 2 * unit, unit, s, 0) for s in range(SIDE)]
    far_parts = product([after(a_far[0], near_parts[0]), a_far[1]], spans, [unit] * SIDE, high, low, "product_far")
    far = direct_reduce([after(far_parts[0], near), *far_parts[1:]])
    q2 = send(far, along_y(2))
    spans = [(0, s * unit, unit, s, 0) for s in range(SIDE)]
    own_parts = product([after(a_own, far_parts[0])], spans, [unit] * SIDE, high, low, "product_own")
    near_theirs = send(jnp.stack([q1[tall:], q3[tall:]]), OTHER_CORE)
    done = finish(where, [q1, q3], near_theirs, row_gap, col_gap, (1, 3))
    own_parts = [after(own_parts[0], far, near_theirs)] + [after(part, near) for part in own_parts[1:]]
    own = direct_reduce(own_parts)

    last_theirs = send(jnp.stack([own[tall:], q2[tall:]]), OTHER_CORE)
    return finish(where, [own, q2], last_theirs, row_gap, col_gap, (0, 2), (done,))


def solution(mesh):
    fine = jax.sharding.Mesh(mesh.devices.reshape(SIDE, SIDE, SIDE, 2), AXES)
    placed = (P(None, AXES, None), P(None, None, AXES), P(None, AXES), P())
    return jax.shard_map(
        per_device, mesh=fine, in_specs=placed, out_specs=P(None, AXES, None), check_vma=False
    )
```

```python
import functools

import jax
import jax.numpy as jnp
from jax import lax
from jax.experimental import pallas as pl
from jax.experimental.pallas import tpu as pltpu
from jax.sharding import PartitionSpec as P

AXES = ("y", "x", "z", "c")
SIDE = 4


def routes(target):
    pairs = []
    for y in range(SIDE):
        for x in range(SIDE):
            for z in range(SIDE):
                for c in range(2):
                    ty, tx, tz, tc = target(y, x, z, c)
                    source = ((y * SIDE + x) * SIDE + z) * 2 + c
                    pairs.append((source, ((ty % SIDE * SIDE + tx % SIDE) * SIDE + tz % SIDE) * 2 + tc % 2))
    return pairs


def along_y(step):
    return routes(lambda y, x, z, c: (y + step, x, z, c))


def along_k(step):
    return routes(lambda y, x, z, c: (y, x, z + step, c) if c == 0 else (y, x + step, z, c))


def along_m(step):
    return routes(lambda y, x, z, c: (y, x + step, z, c) if c == 0 else (y, x, z + step, c))


OTHER_CORE = routes(lambda y, x, z, c: (y, x, z, c + 1))
VMEM_SPEC = pl.BlockSpec(memory_space=pltpu.VMEM)
SMEM_SPEC = pl.BlockSpec(memory_space=pltpu.SMEM)
GRANT = pltpu.CompilerParams(vmem_limit_bytes=20 * 2**20)


def send(value, route):
    return lax.ppermute(value, AXES, route)


def after(value, *earlier):
    return lax.optimization_barrier((value, *earlier))[0]


def ring_near(block, along):
    return send(block, along(1)), send(block, along(-1))


def ring_far(low, high, along):
    half = low.shape[0] // 2
    return send(low[:half], along(1)), send(high[half:], along(-1))


def pack_kernel(where_ref, rows_ref, cols_ref, other_ref, *out_refs):
    c, k_index = where_ref[0], where_ref[1]
    tall, depth = rows_ref.shape[1], out_refs[0].shape[1]
    other_ref[:tall, :] = rows_ref[1 - c]
    other_ref[tall:, :] = cols_ref[1 - c]
    for s, out_ref in enumerate(out_refs):
        span = pl.ds(pl.multiple_of((k_index + s) % SIDE * depth, 128), depth)
        out_ref[:tall, :] = rows_ref[c, :, span]
        out_ref[tall:, :] = cols_ref[c, :, span]


def pack(where, rows, cols):
    height, depth = rows.shape[1] + cols.shape[1], rows.shape[2] // SIDE
    return pl.pallas_call(
        pack_kernel,
        out_shape=[jax.ShapeDtypeStruct((height, depth * SIDE), jnp.float32)]
        + [jax.ShapeDtypeStruct((height, depth), jnp.float32)] * SIDE,
        in_specs=[SMEM_SPEC] + [VMEM_SPEC] * 2,
        out_specs=[VMEM_SPEC] * (1 + SIDE),
        cost_estimate=pl.CostEstimate(flops=0, bytes_accessed=16 * height * depth * SIDE, transcendentals=0),
        compiler_params=GRANT,
        name="pack",
    )(where, rows, cols)


def split_kernel(where_ref, in_ref, *out_refs):
    k_index, depth = where_ref[1], out_refs[0].shape[1]
    for s, out_ref in enumerate(out_refs):
        out_ref[...] = in_ref[:, pl.ds(pl.multiple_of((k_index + s) % SIDE * depth, 128), depth)]


def split(where, value):
    height, depth = value.shape[0], value.shape[1] // SIDE
    return pl.pallas_call(
        split_kernel,
        out_shape=[jax.ShapeDtypeStruct((height, depth), jnp.float32)] * SIDE,
        in_specs=[SMEM_SPEC, VMEM_SPEC],
        out_specs=[VMEM_SPEC] * SIDE,
        cost_estimate=pl.CostEstimate(flops=0, bytes_accessed=8 * height * depth * SIDE, transcendentals=0),
        compiler_params=GRANT,
        name="split",
    )(where, value)


def join_kernel(own, tall, where_ref, *refs):
    c = where_ref[0]
    core = c if own else 1 - c
    a_ref, b_ref = refs[-2:]
    half = refs[0].shape[0] - tall
    for s, ref in enumerate(refs[:SIDE]):
        start = 2 * tall * s + (0 if own else tall)
        a_ref[start : start + tall, :] = ref[:tall, :]
        b_ref[pl.ds(pl.multiple_of(2 * half * s + core * half, 8), half), :] = ref[tall:, :]


def join(where, blocks, tall, into=()):
    height, depth = blocks[0].shape
    shapes = [(2 * tall * SIDE, depth), (2 * (height - tall) * SIDE, depth)]
    return pl.pallas_call(
        functools.partial(join_kernel, not into, tall),
        out_shape=[jax.ShapeDtypeStruct(shape, jnp.float32) for shape in shapes],
        in_specs=[SMEM_SPEC] + [VMEM_SPEC] * (SIDE + len(into)),
        out_specs=[VMEM_SPEC] * 2,
        input_output_aliases={SIDE + 1 + i: i for i in range(len(into))},
        cost_estimate=pl.CostEstimate(flops=0, bytes_accessed=8 * height * depth * SIDE, transcendentals=0),
        compiler_params=GRANT,
        name="join_other" if into else "join_own",
    )(where, *blocks, *into)


def place_kernel(sources, where_ref, *refs):
    refs, high_ref, low_ref = refs[: len(sources)], refs[-2], refs[-1]
    c, k_index, m_index = where_ref[0], where_ref[1], where_ref[2]
    for ref, (t, first, count) in zip(refs, sources):
        wide = ref.shape[0] // count
        m = (m_index - t + SIDE) % SIDE

        def body(i, carry, ref=ref, m=m, first=first):
            k = (k_index - i - first + SIDE) % SIDE
            row = jnp.where(c == 0, m * SIDE + k, k * SIDE + m) * wide
            block = ref[pl.ds(pl.multiple_of(i * wide, 8), wide), :]
            high = block.astype(jnp.bfloat16)
            low = (block - high.astype(jnp.float32)).astype(jnp.bfloat16)
            high_ref[pl.ds(pl.multiple_of(row, 16), wide), :] = high
            low_ref[pl.ds(pl.multiple_of(row, 16), wide), :] = low
            return carry

        lax.fori_loop(0, count, body, 0, unroll=True)


def place(where, blocks, sources, total, into=()):
    depth = blocks[0].shape[1]
    size = sum(block.shape[0] for block in blocks) * depth
    n = len(blocks)
    return pl.pallas_call(
        functools.partial(place_kernel, sources),
        out_shape=[jax.ShapeDtypeStruct((total, depth), jnp.bfloat16)] * 2,
        in_specs=[SMEM_SPEC] + [VMEM_SPEC] * (n + len(into)),
        out_specs=[VMEM_SPEC] * 2,
        input_output_aliases={n + 1 + i: i for i in range(len(into))},
        cost_estimate=pl.CostEstimate(flops=4 * size, bytes_accessed=8 * size, transcendentals=0),
        compiler_params=GRANT,
        name="place_far" if into else "place_near",
    )(where, *blocks, *into)


def product_kernel(spans, n_in, *refs):
    a_refs, (high_ref, low_ref), rest = refs[:n_in], refs[n_in : n_in + 2], refs[n_in + 2 :]
    out_refs, (a_ref,) = rest[:-1], rest[-1:]
    rows = a_ref.shape[0] // 2
    at = 0
    for source, first, count, _, _ in spans:
        value = a_refs[source][first : first + count, :]
        high = value.astype(jnp.bfloat16)
        a_ref[at : at + count, :] = high
        a_ref[rows + at : rows + at + count, :] = (value - high.astype(jnp.float32)).astype(jnp.bfloat16)
        at += count
    tile = 256
    dims = (((1,), (1,)), ((), ()))

    def body(j, carry):
        cols = pl.ds(pl.multiple_of(j * tile, tile), tile)
        both = lax.dot_general(a_ref[...], high_ref[cols, :], dims, preferred_element_type=jnp.float32)
        rest_of = lax.dot_general(a_ref[:rows, :], low_ref[cols, :], dims, preferred_element_type=jnp.float32)
        value = both[:rows] + (both[rows:] + rest_of)
        at = 0
        for _, _, count, out, out_first in spans:
            out_refs[out][out_first : out_first + count, cols] = value[at : at + count]
            at += count
        return carry

    lax.fori_loop(0, high_ref.shape[0] // tile, body, 0, unroll=True)


def product(sources, spans, out_rows, high, low, name):
    width, depth = high.shape
    rows = sum(span[2] for span in spans)
    return pl.pallas_call(
        functools.partial(product_kernel, spans, len(sources)),
        out_shape=[jax.ShapeDtypeStruct((count, width), jnp.float32) for count in out_rows],
        in_specs=[VMEM_SPEC] * (len(sources) + 2),
        out_specs=[VMEM_SPEC] * len(out_rows),
        scratch_shapes=[pltpu.VMEM((2 * rows, depth), jnp.bfloat16)],
        cost_estimate=pl.CostEstimate(
            flops=6 * rows * width * depth, bytes_accessed=4 * (rows * (width + depth) + width * depth), transcendentals=0
        ),
        compiler_params=GRANT,
        name=name,
    )(*sources, high, low)


def direct_reduce(parts):
    p0, p1, p2, p3 = parts
    return p0 + send(p1, along_k(-1)) + send(p3, along_k(1)) + send(p2, along_k(2))


def finish_kernel(turns, where_ref, *refs):
    mine_refs, (theirs_ref, row_ref, col_ref) = refs[:2], refs[2:5]
    out_ref, value_ref, sems = refs[-3:]
    c, y = where_ref[0], where_ref[3]
    half, width = theirs_ref.shape[1:]
    copies = []
    for i, t in enumerate(turns):
        cols = pl.ds(pl.multiple_of((y + t) % SIDE * width, 128), width)
        for j, (g, value) in enumerate(((c, mine_refs[i][:half, :]), (1 - c, theirs_ref[i]))):
            value_ref[i, j] = value / (row_ref[g] + col_ref[g, :, cols])
            copies.append(pltpu.make_async_copy(value_ref.at[i, j], out_ref.at[g, :, cols], sems.at[i, j]))
            copies[-1].start()
    for copy in copies:
        copy.wait()


def finish(where, mine, theirs, row_gap, col_gap, turns, into=()):
    _, half, width = theirs.shape
    size = 4 * half * width
    return pl.pallas_call(
        functools.partial(finish_kernel, turns),
        out_shape=jax.ShapeDtypeStruct((2, half, SIDE * width), jnp.float32),
        in_specs=[SMEM_SPEC] + [VMEM_SPEC] * 5 + [pl.BlockSpec(memory_space=pl.ANY)] * len(into),
        out_specs=pl.BlockSpec(memory_space=pl.ANY),
        scratch_shapes=[pltpu.VMEM((2, 2, half, width), jnp.float32), pltpu.SemaphoreType.DMA((2, 2))],
        input_output_aliases={6: 0} if into else {},
        cost_estimate=pl.CostEstimate(flops=3 * size, bytes_accessed=8 * size, transcendentals=0),
        compiler_params=GRANT,
        name="finish_last" if into else "finish_near",
    )(where, *mine, theirs, row_gap, col_gap, *into)


def per_device(amplitudes, integrals, row_gap, col_gap):
    y, x, z, c = (lax.axis_index(name) for name in AXES)
    k_index = jnp.where(c == 0, z, x)
    m_index = jnp.where(c == 0, x, z)
    where = jnp.stack([c, k_index, m_index, y]).astype(jnp.int32)
    columns = jnp.swapaxes(integrals, 1, 2)

    tall = amplitudes.shape[1]
    other, *packed = pack(where, amplitudes, columns)
    other_packed = split(where, send(other, OTHER_CORE))
    own_moved, other_moved = (
        [blocks[0]] + [send(blocks[s], along_k(s)) for s in (1, 2, 3)] for blocks in (packed, other_packed)
    )
    a_own, b_own = join(where, other_moved, tall, join(where, own_moved, tall))

    a_near = ring_near(a_own, along_y)
    b_near = ring_near(b_own, along_m)
    b_far = ring_far(*b_near, along_m)
    total = b_own.shape[0] * SIDE
    where, row_gap, col_gap = lax.optimization_barrier((where, row_gap[:, :, None], col_gap[:, None, :]))
    placed = place(where, [b_own, *b_near], [(0, 0, 4), (1, 0, 4), (3, 0, 4)], total)
    a_near, placed = lax.optimization_barrier((a_near, placed))
    a_far = ring_far(*a_near, along_y)
    high, low = place(where, b_far, [(2, 0, 2), (2, 2, 2)], total, placed)

    unit = 2 * tall
    spans = [(t, s * unit, unit, s, t * unit) for t in range(2) for s in range(SIDE)]
    near_parts = product(a_near, spans, [2 * unit] * SIDE, high, low, "product_near")
    near = direct_reduce(near_parts)
    q1 = send(near[:unit], along_y(-1))
    q3 = send(near[unit:], along_y(1))
    spans = [(s // 2, s % 2 * unit, unit, s, 0) for s in range(SIDE)]
    far_parts = product([after(a_far[0], near_parts[0]), a_far[1]], spans, [unit] * SIDE, high, low, "product_far")
    far = direct_reduce([after(far_parts[0], near), *far_parts[1:]])
    q2 = send(far, along_y(2))
    spans = [(0, s * unit, unit, s, 0) for s in range(SIDE)]
    own_parts = product([after(a_own, far_parts[0])], spans, [unit] * SIDE, high, low, "product_own")
    near_theirs = send(jnp.stack([q1[tall:], q3[tall:]]), OTHER_CORE)
    done = finish(where, [q1, q3], near_theirs, row_gap, col_gap, (1, 3))
    own_parts = [after(own_parts[0], far, near_theirs)] + [after(part, near) for part in own_parts[1:]]
    own = direct_reduce(own_parts)

    last_theirs = send(jnp.stack([own[tall:], q2[tall:]]), OTHER_CORE)
    return finish(where, [own, q2], last_theirs, row_gap, col_gap, (0, 2), (done,))


def solution(mesh):
    fine = jax.sharding.Mesh(mesh.devices.reshape(SIDE, SIDE, SIDE, 2), AXES)
    placed = (P(None, AXES, None), P(None, None, AXES), P(None, AXES), P())
    return jax.shard_map(
        per_device, mesh=fine, in_specs=placed, out_specs=P(None, AXES, None), check_vma=False
    )
```

```python
import functools

import jax
import jax.numpy as jnp
from jax import lax
from jax.experimental import pallas as pl
from jax.experimental.pallas import tpu as pltpu
from jax.sharding import PartitionSpec as P

AXES = ("y", "x", "z", "c")
SIDE = 4


def routes(target):
    pairs = []
    for y in range(SIDE):
        for x in range(SIDE):
            for z in range(SIDE):
                for c in range(2):
                    ty, tx, tz, tc = target(y, x, z, c)
                    source = ((y * SIDE + x) * SIDE + z) * 2 + c
                    pairs.append((source, ((ty % SIDE * SIDE + tx % SIDE) * SIDE + tz % SIDE) * 2 + tc % 2))
    return pairs


def along_y(step):
    return routes(lambda y, x, z, c: (y + step, x, z, c))


def along_k(step):
    return routes(lambda y, x, z, c: (y, x, z + step, c) if c == 0 else (y, x + step, z, c))


def along_m(step):
    return routes(lambda y, x, z, c: (y, x + step, z, c) if c == 0 else (y, x, z + step, c))


OTHER_CORE = routes(lambda y, x, z, c: (y, x, z, c + 1))
VMEM_SPEC = pl.BlockSpec(memory_space=pltpu.VMEM)
SMEM_SPEC = pl.BlockSpec(memory_space=pltpu.SMEM)
GRANT = pltpu.CompilerParams(vmem_limit_bytes=14 * 2**20)


def send(value, route):
    return lax.ppermute(value, AXES, route)


def after(value, *earlier):
    return lax.optimization_barrier((value, *earlier))[0]


def ring_near(block, along):
    return send(block, along(1)), send(block, along(-1))


def ring_far(low, high, along):
    half = low.shape[0] // 2
    return send(low[:half], along(1)), send(high[half:], along(-1))


def pack_kernel(where_ref, rows_ref, cols_ref, other_ref, *out_refs):
    c, k_index = where_ref[0], where_ref[1]
    tall, depth = rows_ref.shape[1], out_refs[0].shape[1]
    other_ref[:tall, :] = rows_ref[1 - c]
    other_ref[tall:, :] = cols_ref[1 - c]
    for s, out_ref in enumerate(out_refs):
        span = pl.ds(pl.multiple_of((k_index + s) % SIDE * depth, 128), depth)
        out_ref[:tall, :] = rows_ref[c, :, span]
        out_ref[tall:, :] = cols_ref[c, :, span]


def pack(where, rows, cols):
    height, depth = rows.shape[1] + cols.shape[1], rows.shape[2] // SIDE
    return pl.pallas_call(
        pack_kernel,
        out_shape=[jax.ShapeDtypeStruct((height, depth * SIDE), jnp.float32)]
        + [jax.ShapeDtypeStruct((height, depth), jnp.float32)] * SIDE,
        in_specs=[SMEM_SPEC] + [VMEM_SPEC] * 2,
        out_specs=[VMEM_SPEC] * (1 + SIDE),
        cost_estimate=pl.CostEstimate(flops=0, bytes_accessed=16 * height * depth * SIDE, transcendentals=0),
        compiler_params=GRANT,
        name="pack",
    )(where, rows, cols)


def split_kernel(where_ref, in_ref, *out_refs):
    k_index, depth = where_ref[1], out_refs[0].shape[1]
    for s, out_ref in enumerate(out_refs):
        out_ref[...] = in_ref[:, pl.ds(pl.multiple_of((k_index + s) % SIDE * depth, 128), depth)]


def split(where, value):
    height, depth = value.shape[0], value.shape[1] // SIDE
    return pl.pallas_call(
        split_kernel,
        out_shape=[jax.ShapeDtypeStruct((height, depth), jnp.float32)] * SIDE,
        in_specs=[SMEM_SPEC, VMEM_SPEC],
        out_specs=[VMEM_SPEC] * SIDE,
        cost_estimate=pl.CostEstimate(flops=0, bytes_accessed=8 * height * depth * SIDE, transcendentals=0),
        compiler_params=GRANT,
        name="split",
    )(where, value)


def join_kernel(own, tall, where_ref, *refs):
    c = where_ref[0]
    core = c if own else 1 - c
    a_ref, b_ref = refs[-2:]
    half = refs[0].shape[0] - tall
    for s, ref in enumerate(refs[:SIDE]):
        start = 2 * tall * s + (0 if own else tall)
        a_ref[start : start + tall, :] = ref[:tall, :]
        b_ref[pl.ds(pl.multiple_of(2 * half * s + core * half, 8), half), :] = ref[tall:, :]


def join(where, blocks, tall, into=()):
    height, depth = blocks[0].shape
    shapes = [(2 * tall * SIDE, depth), (2 * (height - tall) * SIDE, depth)]
    return pl.pallas_call(
        functools.partial(join_kernel, not into, tall),
        out_shape=[jax.ShapeDtypeStruct(shape, jnp.float32) for shape in shapes],
        in_specs=[SMEM_SPEC] + [VMEM_SPEC] * (SIDE + len(into)),
        out_specs=[VMEM_SPEC] * 2,
        input_output_aliases={SIDE + 1 + i: i for i in range(len(into))},
        cost_estimate=pl.CostEstimate(flops=0, bytes_accessed=8 * height * depth * SIDE, transcendentals=0),
        compiler_params=GRANT,
        name="join_other" if into else "join_own",
    )(where, *blocks, *into)


def place_kernel(sources, where_ref, *refs):
    refs, high_ref, low_ref = refs[: len(sources)], refs[-2], refs[-1]
    c, k_index, m_index = where_ref[0], where_ref[1], where_ref[2]
    for ref, (t, first, count) in zip(refs, sources):
        wide = ref.shape[0] // count
        m = (m_index - t + SIDE) % SIDE

        def body(i, carry, ref=ref, m=m, first=first):
            k = (k_index - i - first + SIDE) % SIDE
            row = jnp.where(c == 0, m * SIDE + k, k * SIDE + m) * wide
            block = ref[pl.ds(pl.multiple_of(i * wide, 8), wide), :]
            high = block.astype(jnp.bfloat16)
            low = (block - high.astype(jnp.float32)).astype(jnp.bfloat16)
            high_ref[pl.ds(pl.multiple_of(row, 16), wide), :] = high
            low_ref[pl.ds(pl.multiple_of(row, 16), wide), :] = low
            return carry

        lax.fori_loop(0, count, body, 0, unroll=True)


def place(where, blocks, sources, total, into=()):
    depth = blocks[0].shape[1]
    size = sum(block.shape[0] for block in blocks) * depth
    n = len(blocks)
    return pl.pallas_call(
        functools.partial(place_kernel, sources),
        out_shape=[jax.ShapeDtypeStruct((total, depth), jnp.bfloat16)] * 2,
        in_specs=[SMEM_SPEC] + [VMEM_SPEC] * (n + len(into)),
        out_specs=[VMEM_SPEC] * 2,
        input_output_aliases={n + 1 + i: i for i in range(len(into))},
        cost_estimate=pl.CostEstimate(flops=4 * size, bytes_accessed=8 * size, transcendentals=0),
        compiler_params=GRANT,
        name="place_far" if into else "place_near",
    )(where, *blocks, *into)


def product_kernel(spans, n_in, *refs):
    a_refs, (high_ref, low_ref), rest = refs[:n_in], refs[n_in : n_in + 2], refs[n_in + 2 :]
    out_refs, (a_ref,) = rest[:-1], rest[-1:]
    rows = a_ref.shape[0] // 2
    at = 0
    for source, first, count, _, _ in spans:
        value = a_refs[source][first : first + count, :]
        high = value.astype(jnp.bfloat16)
        a_ref[at : at + count, :] = high
        a_ref[rows + at : rows + at + count, :] = (value - high.astype(jnp.float32)).astype(jnp.bfloat16)
        at += count
    tile = 256
    dims = (((1,), (1,)), ((), ()))

    def body(j, carry):
        cols = pl.ds(pl.multiple_of(j * tile, tile), tile)
        both = lax.dot_general(a_ref[...], high_ref[cols, :], dims, preferred_element_type=jnp.float32)
        rest_of = lax.dot_general(a_ref[:rows, :], low_ref[cols, :], dims, preferred_element_type=jnp.float32)
        value = both[:rows] + (both[rows:] + rest_of)
        at = 0
        for _, _, count, out, out_first in spans:
            out_refs[out][out_first : out_first + count, cols] = value[at : at + count]
            at += count
        return carry

    lax.fori_loop(0, high_ref.shape[0] // tile, body, 0, unroll=True)


def product(sources, spans, out_rows, high, low, name):
    width, depth = high.shape
    rows = sum(span[2] for span in spans)
    return pl.pallas_call(
        functools.partial(product_kernel, spans, len(sources)),
        out_shape=[jax.ShapeDtypeStruct((count, width), jnp.float32) for count in out_rows],
        in_specs=[VMEM_SPEC] * (len(sources) + 2),
        out_specs=[VMEM_SPEC] * len(out_rows),
        scratch_shapes=[pltpu.VMEM((2 * rows, depth), jnp.bfloat16)],
        cost_estimate=pl.CostEstimate(
            flops=6 * rows * width * depth, bytes_accessed=4 * (rows * (width + depth) + width * depth), transcendentals=0
        ),
        compiler_params=GRANT,
        name=name,
    )(*sources, high, low)


def direct_reduce(parts):
    p0, p1, p2, p3 = parts
    return p0 + send(p1, along_k(-1)) + send(p3, along_k(1)) + send(p2, along_k(2))


def finish_kernel(turns, where_ref, *refs):
    mine_refs, (theirs_ref, row_ref, col_ref) = refs[:2], refs[2:5]
    out_ref, value_ref, sems = refs[-3:]
    c, y = where_ref[0], where_ref[3]
    half, width = theirs_ref.shape[1:]
    copies = []
    for i, t in enumerate(turns):
        cols = pl.ds(pl.multiple_of((y + t) % SIDE * width, 128), width)
        for j, (g, value) in enumerate(((c, mine_refs[i][:half, :]), (1 - c, theirs_ref[i]))):
            value_ref[i, j] = value / (row_ref[g] + col_ref[g, :, cols])
            copies.append(pltpu.make_async_copy(value_ref.at[i, j], out_ref.at[g, :, cols], sems.at[i, j]))
            copies[-1].start()
    for copy in copies:
        copy.wait()


def finish(where, mine, theirs, row_gap, col_gap, turns, into=()):
    _, half, width = theirs.shape
    size = 4 * half * width
    return pl.pallas_call(
        functools.partial(finish_kernel, turns),
        out_shape=jax.ShapeDtypeStruct((2, half, SIDE * width), jnp.float32),
        in_specs=[SMEM_SPEC] + [VMEM_SPEC] * 5 + [pl.BlockSpec(memory_space=pl.ANY)] * len(into),
        out_specs=pl.BlockSpec(memory_space=pl.ANY),
        scratch_shapes=[pltpu.VMEM((2, 2, half, width), jnp.float32), pltpu.SemaphoreType.DMA((2, 2))],
        input_output_aliases={6: 0} if into else {},
        cost_estimate=pl.CostEstimate(flops=3 * size, bytes_accessed=8 * size, transcendentals=0),
        compiler_params=GRANT,
        name="finish_last" if into else "finish_near",
    )(where, *mine, theirs, row_gap, col_gap, *into)


def per_device(amplitudes, integrals, row_gap, col_gap):
    y, x, z, c = (lax.axis_index(name) for name in AXES)
    k_index = jnp.where(c == 0, z, x)
    m_index = jnp.where(c == 0, x, z)
    where = jnp.stack([c, k_index, m_index, y]).astype(jnp.int32)
    columns = jnp.swapaxes(integrals, 1, 2)

    tall = amplitudes.shape[1]
    other, *packed = pack(where, amplitudes, columns)
    other_packed = split(where, send(other, OTHER_CORE))
    own_moved, other_moved = (
        [blocks[0]] + [send(blocks[s], along_k(s)) for s in (1, 2, 3)] for blocks in (packed, other_packed)
    )
    a_own, b_own = join(where, other_moved, tall, join(where, own_moved, tall))

    a_near = ring_near(a_own, along_y)
    b_near = ring_near(b_own, along_m)
    b_far = ring_far(*b_near, along_m)
    total = b_own.shape[0] * SIDE
    where, row_gap, col_gap = lax.optimization_barrier((where, row_gap[:, :, None], col_gap[:, None, :]))
    placed = place(where, [b_own, *b_near], [(0, 0, 4), (1, 0, 4), (3, 0, 4)], total)
    a_near, placed = lax.optimization_barrier((a_near, placed))
    a_far = ring_far(*a_near, along_y)
    high, low = place(where, b_far, [(2, 0, 2), (2, 2, 2)], total, placed)

    unit = 2 * tall
    spans = [(t, s * unit, unit, s, t * unit) for t in range(2) for s in range(SIDE)]
    near_parts = product(a_near, spans, [2 * unit] * SIDE, high, low, "product_near")
    near = direct_reduce(near_parts)
    q1 = send(near[:unit], along_y(-1))
    q3 = send(near[unit:], along_y(1))
    spans = [(s // 2, s % 2 * unit, unit, s, 0) for s in range(SIDE)]
    far_parts = product([after(a_far[0], near_parts[0]), a_far[1]], spans, [unit] * SIDE, high, low, "product_far")
    far = direct_reduce([after(far_parts[0], near), *far_parts[1:]])
    q2 = send(far, along_y(2))
    spans = [(0, s * unit, unit, s, 0) for s in range(SIDE)]
    own_parts = product([after(a_own, far_parts[0])], spans, [unit] * SIDE, high, low, "product_own")
    near_theirs = send(jnp.stack([q1[tall:], q3[tall:]]), OTHER_CORE)
    done = finish(where, [q1, q3], near_theirs, row_gap, col_gap, (1, 3))
    own_parts = [after(own_parts[0], far, near_theirs)] + [after(part, near) for part in own_parts[1:]]
    own = direct_reduce(own_parts)

    last_theirs = send(jnp.stack([own[tall:], q2[tall:]]), OTHER_CORE)
    return finish(where, [own, q2], last_theirs, row_gap, col_gap, (0, 2), (done,))


def solution(mesh):
    fine = jax.sharding.Mesh(mesh.devices.reshape(SIDE, SIDE, SIDE, 2), AXES)
    placed = (P(None, AXES, None), P(None, None, AXES), P(None, AXES), P())
    return jax.shard_map(
        per_device, mesh=fine, in_specs=placed, out_specs=P(None, AXES, None), check_vma=False
    )
```
